256 devices in a mesh: row: 16 (over y_hi, x, core), col: 16 (over y_lo, z).
Axes of the slice: x: 4, y: 4 (y_hi: 2, y_lo: 2; y = y_hi * 2 + y_lo), z: 8, core: 2. Of those that a mesh axis runs over, the one named last changes fastest.
Arguments:
- pool: bfloat16 [32768, 128], P(('row', 'col')), may hold values from -6 to 6
- targets: bfloat16 [32768], P(('row', 'col')), may hold values from -15 to 15
- picks: int32 [4096], P(('row', 'col')), may hold values from 0 to 127
- inducing: float32 [8192, 128], replicated, may hold values from -6 to 6
- inv_sq_lengths: float32 [128], replicated, may hold values from 0.04 to 0.12
- prec_old: float32 [8192, 8192], P('row', 'col'), may hold values from -1 to 6, as said below
- mean_old: float32 [8192], P('row'), may hold values from -6 to 6
- panel: int32 [1], replicated, may hold values from 0 to 31
Outputs:
- prec_new: float32 [8192, 8192], P('row', 'col')
- mean_new: float32 [8192], P('row')
The draws below stay inside these ranges and needn't reach their ends.
Inputs may be any that keep to these rules, and one draw needn't show every extreme that they name: `picks`: each entry indexes a row of the dataset block held by the same device as the entry. `prec_old`: symmetric and positive definite.
All inputs are finite; a program needn't handle non-finite values.
Results may differ from the reference program's by a relative error of at most 0.0028.
Values may be sent and summed in bfloat16 or wider, within the bound.
No kernel may reach another device: no remote copies, remote signals or barrier semaphores. Data moves between devices by JAX's collectives and lax.ppermute only.
A program may use at most 128 MiB of HBM per device.

```python
import math
import jax
import jax.numpy as jnp
from jax import lax

M = 8192
F = 128
PB = 256
B_DEV = 16
POOL_DEV = 128
B_TOTAL = 4096
POOL_TOTAL = 32768


def draw_targets(key, part):
    ramp = jnp.exp(jnp.log(3.0) * jnp.arange(POOL_TOTAL, dtype=jnp.float32) / max(POOL_TOTAL - 1, 1))
    noise = jax.random.normal(key, (POOL_TOTAL,), jnp.float32)
    raw = noise * ramp
    low = jnp.min(raw)
    high = jnp.max(raw)
    scaled = 30.0 * (raw - low) / (high - low) - 15.0
    return jnp.clip(scaled, -15.0, 15.0).astype(jnp.bfloat16)


def draw_prec_old(key, part):
    base_key = jax.random.fold_in(key, 11)
    diag_key = jax.random.fold_in(key, 12)
    base = jax.random.normal(base_key, (M, M), jnp.float32)
    diag_vals = jax.random.uniform(diag_key, (M,), jnp.float32, 3.0, 4.0)
    symmetric = (base + base.T) / jnp.sqrt(2.0 * M)
    symmetric = jnp.clip(symmetric, -0.9, 0.9)
    return symmetric + jnp.diag(diag_vals)


def with_ends(result, rng, least, largest):
    dims = result.shape
    index_at = [jax.random.randint(jax.random.fold_in(rng, axis), (), 0, dims[axis]) for axis in range(len(dims))]
    result = result.at[tuple(index_at)].set(least)
    longest = dims.index(max(dims))
    index_at[longest] = (index_at[longest] + 1) % dims[longest]
    return result.at[tuple(index_at)].set(largest)


def level_of(stream_key, dims, split, smallest, top_value):
    def one(axis_at, blocks):
        draws = jax.random.uniform(jax.random.fold_in(jax.random.fold_in(stream_key, 6), axis_at), (blocks,), jnp.float32, smallest / len(split), top_value / len(split))
        return jnp.repeat(jnp.exp(draws), dims[axis_at] // blocks).reshape((-1,) + (1,) * (len(dims) - axis_at - 1))

    factor_of = one(*split[0])
    for cut in split[1:]:
        factor_of = factor_of * one(*cut)
    return factor_of


def scatter_about(stream_key, shape, deviation, bound, shards=(), held_as=jnp.bfloat16):
    array = deviation * jax.random.normal(stream_key, shape, jnp.float32)
    if shards:
        array = array * level_of(stream_key, shape, shards, -0.22, 0.18)
    return jnp.clip(array, -bound, bound).astype(held_as)


def setup_inputs(seed: int = 0) -> dict:
    streams_of = jax.random.split(jax.random.key(seed), 9)
    return {
        "pool": scatter_about(streams_of[0], (POOL_TOTAL, F), 1.0, 6.0, ((0, 256),)),
        "targets": draw_targets(jax.random.fold_in(streams_of[8], 71), 0),
        "picks": with_ends(jax.random.randint(streams_of[2], (B_TOTAL,), 0, POOL_DEV), jax.random.fold_in(streams_of[2], 1), 0, POOL_DEV - 1).astype(jnp.int32),
        "inducing": scatter_about(streams_of[3], (M, F), 1.0, 6.0, (), jnp.float32),
        "inv_sq_lengths": jnp.clip(jnp.exp(jax.random.uniform(streams_of[4], (F,), jnp.float32, math.log(0.04), math.log(0.12))), 0.04, 0.12),
        "prec_old": draw_prec_old(jax.random.fold_in(streams_of[8], 71), 0),
        "mean_old": scatter_about(streams_of[6], (M,), 1.0, 6.0, ((0, 16),), jnp.float32),
        "panel": jax.random.randint(streams_of[7], (1,), 0, M // PB).astype(jnp.int32),
    }


RATE = 0.5
EPSILON = 1e-05

def kernel_block(points, weights, sample_x):
    sample_f = sample_x.astype(jnp.float32)
    point_sq = lax.optimization_barrier(jnp.sum(points * points * weights, axis=1))
    sample_sq = lax.optimization_barrier(jnp.sum(sample_f * sample_f * weights, axis=1))
    cross_term = lax.dot_general(points * weights, sample_f, (((1,), (1,)), ((), ())), precision=lax.Precision.HIGHEST)
    return jnp.exp(-0.5 * (point_sq[:, None] + sample_sq[None, :] - 2.0 * cross_term)).astype(jnp.bfloat16)

def reference(pool, targets, picks, inducing, inv_sq_lengths, prec_old, mean_old, panel):
    owner_dev = jnp.arange(B_TOTAL, dtype=jnp.int32) // B_DEV
    pool_rows = (owner_dev * POOL_DEV + picks).astype(jnp.int32)
    sample_x = pool[pool_rows]
    sample_y = targets[pool_rows].astype(jnp.float32)
    features = kernel_block(inducing, inv_sq_lengths, sample_x).astype(jnp.float32)
    gram_full = jnp.dot(features, features.T, precision=lax.Precision.HIGHEST)
    fit_full = jnp.dot(features, sample_y, precision=lax.Precision.HIGHEST)
    power_sum = jnp.sum(sample_y * sample_y)
    trace_scale = jnp.trace(gram_full) / M
    joined = (1.0 - RATE) * prec_old + RATE * gram_full / trace_scale
    mean_mid = (1.0 - RATE) * mean_old + RATE * fit_full / jnp.sqrt(trace_scale * (power_sum / B_TOTAL + EPSILON))
    panel_start = (panel[0] * PB).astype(jnp.int32)
    zero_index = jnp.zeros((), jnp.int32)
    diag_block = lax.dynamic_slice(joined, (panel_start, panel_start), (PB, PB))
    factor = jnp.linalg.cholesky(diag_block)
    column_panel = lax.dynamic_slice(joined, (zero_index, panel_start), (M, PB))
    wide_rows = lax.linalg.triangular_solve(factor, column_panel, left_side=False, lower=True, transpose_a=True)
    mean_part = lax.dynamic_slice(mean_mid, (panel_start,), (PB,))
    head_part = lax.linalg.triangular_solve(factor, mean_part[:, None], left_side=True, lower=True)[:, 0]
    updated = joined - jnp.dot(wide_rows, wide_rows.T, precision=lax.Precision.HIGHEST)
    updated = lax.dynamic_update_slice(updated, wide_rows, (zero_index, panel_start))
    updated = lax.dynamic_update_slice(updated, wide_rows.T, (panel_start, zero_index))
    updated = lax.dynamic_update_slice(updated, factor, (panel_start, panel_start))
    mean_next = mean_mid - jnp.dot(wide_rows, head_part, precision=lax.Precision.HIGHEST)
    mean_next = lax.dynamic_update_slice(mean_next, head_part, (panel_start,))
    return (updated, mean_next)
```

```python
import functools
import math

import jax
import jax.numpy as jnp
from jax import lax
from jax.experimental import pallas as pl
from jax.experimental.pallas import tpu as pltpu
from jax.sharding import Mesh
from jax.sharding import PartitionSpec as P

M = 8192
F = 128
PB = 256
TILE = 512
B_TOTAL = 4096
HALF = 2048
CHUNK = 512
ROW = ("yh", "x", "core")
COL = ("yl", "z")
XY = ("yh", "x", "yl")
ALL = ROW + COL
RATE = 0.5
EPSILON = 1e-05
LOG2E = math.log2(math.e)
F32 = jnp.float32
BF16 = jnp.bfloat16
NT = (((1,), (1,)), ((), ()))
HIGHEST = lax.Precision.HIGHEST


def swapped(value, axis, size, bit):
    return lax.ppermute(value, axis, [(i, i ^ bit) for i in range(size)])


def split2(value):
    high = lax.reduce_precision(value, 8, 7)
    return high.astype(BF16), (value - high).astype(BF16)


def split3(value):
    high = lax.reduce_precision(value, 8, 7)
    rest = value - high
    mid = lax.reduce_precision(rest, 8, 7)
    return high.astype(BF16), mid.astype(BF16), (rest - mid).astype(BF16)


def packed(value):
    high, low = split2(value)
    return jnp.concatenate([high[..., :128], high[..., 128:], low[..., :128], low[..., 128:]], axis=-2)


def unpacked(rows):
    n = rows.shape[-2] // 4
    q = rows.astype(F32)
    left = q[..., :n, :] + q[..., 2 * n : 3 * n, :]
    right = q[..., n : 2 * n, :] + q[..., 3 * n :, :]
    return jnp.concatenate([left, right], axis=-1)


def joined_along(value, axis, size, bit, at):
    other = swapped(value, axis, size, bit)
    mine_first = (lax.axis_index(axis) // bit) % 2 == 0
    first = jnp.where(mine_first, value, other)
    second = jnp.where(mine_first, other, value)
    return jnp.stack([first, second], axis=at)


def rows_in_order(chunks):
    return chunks.reshape(8, 2, 32, PB).transpose(1, 0, 2, 3).reshape(TILE, PB)


def own_trace(inducing, weights, samples):
    sample_f = samples.astype(F32)
    point_sq = lax.dot_general(weights[None, :], inducing * inducing, NT, precision=HIGHEST)
    sample_sq = jnp.sum(sample_f * sample_f * weights, axis=1)
    cross = lax.dot_general(sample_f * weights, inducing, NT, precision=HIGHEST)
    feat = jnp.exp(-0.5 * (point_sq + sample_sq[:, None] - 2.0 * cross))
    feat = lax.reduce_precision(feat, 8, 7)
    return jnp.sum(feat * feat)


def pieces(value):
    high = value.astype(BF16)
    rest = value - high.astype(F32)
    mid = rest.astype(BF16)
    return high, mid, (rest - mid.astype(F32)).astype(BF16)


def gram_kernel(first, idx_ref, pr_ref, pc_ref, pp_ref, w_ref, x_ref, y_ref, *refs):
    if first:
        grc_ref, gp_ref, fit_ref, paug, xaug = refs
    else:
        grc_in, gp_in, fit_in, grc_ref, gp_ref, fit_ref, paug, xaug = refs
    step = pl.program_id(0)
    lane = lax.broadcasted_iota(jnp.int32, (1, 128), 1)

    @pl.when(step == 0)
    def _():
        w = w_ref[...]
        at = 0
        for ref in (pr_ref, pc_ref, pp_ref):
            pts = ref[...]
            n = pts.shape[0]
            p1, p2, p3 = pieces(pts * w * LOG2E)
            sq = jnp.sum(pts * pts * w, axis=1, keepdims=True) * (-0.5 * LOG2E)
            s1, s2, s3 = (s.astype(F32) for s in pieces(sq))
            extra = jnp.where(lane == 0, s1, jnp.where(lane == 1, s2, jnp.where(lane == 2, s3, 0.0)))
            extra = extra + jnp.where((lane >= 3) & (lane < 6), 1.0, 0.0)
            paug[at : at + n, 0:128] = p1
            paug[at : at + n, 128:256] = p2
            paug[at : at + n, 256:384] = p3
            paug[at : at + n, 384:512] = extra.astype(BF16)
            at += n
        if first:
            grc_ref[...] = jnp.zeros_like(grc_ref)
            gp_ref[...] = jnp.zeros_like(gp_ref)
            fit_ref[...] = jnp.zeros_like(fit_ref)
        else:
            grc_ref[...] = grc_in[...]
            gp_ref[...] = gp_in[...]
            fit_ref[...] = fit_in[...]

    x = x_ref[...]
    xf = x.astype(F32)
    sq = jnp.sum(xf * xf * w_ref[...], axis=1, keepdims=True) * (-0.5 * LOG2E)
    s1, s2, s3 = (s.astype(F32) for s in pieces(sq))
    extra = jnp.where(lane == 3, s1, jnp.where(lane == 4, s2, jnp.where(lane == 5, s3, 0.0)))
    extra = extra + jnp.where(lane < 3, 1.0, 0.0)
    xaug[:, 0:128] = x
    xaug[:, 128:256] = x
    xaug[:, 256:384] = x
    xaug[:, 384:512] = extra.astype(BF16)
    xa = xaug[...]

    def feats(at, n):
        e = lax.dot_general(paug[at : at + n, :], xa, NT, preferred_element_type=F32)
        return jnp.exp2(e).astype(BF16)

    f_r = feats(0, TILE)
    f_c = feats(TILE, TILE)
    f_p = feats(2 * TILE, PB)
    grc_ref[...] += lax.dot_general(f_r, f_c, NT, preferred_element_type=F32)
    gp_ref[0:TILE, :] += lax.dot_general(f_r, f_p, NT, preferred_element_type=F32)
    gp_ref[TILE : 2 * TILE, :] += lax.dot_general(f_c, f_p, NT, preferred_element_type=F32)
    gp_ref[2 * TILE :, :] += lax.dot_general(f_p, f_p, NT, preferred_element_type=F32)
    y = y_ref[...].reshape(CHUNK // 128, 128).astype(F32)
    for at, f in ((0, f_r), (TILE, f_p)):
        acc = fit_ref[at : at + f.shape[0], :]
        for k in range(CHUNK // 128):
            acc = acc + f[:, 128 * k : 128 * (k + 1)].astype(F32) * y[k : k + 1, :]
        fit_ref[at : at + f.shape[0], :] = acc


def gram_part(idx, inducing, weights, x, y, carry):
    first = carry is None
    whole = lambda shape: pl.BlockSpec(shape, lambda i, idx: (0,) * len(shape))
    shapes = ((TILE, TILE), (2 * TILE + PB, PB), (TILE + PB, 128))
    in_specs = [
        pl.BlockSpec((TILE, F), lambda i, idx: (idx[0], 0)),
        pl.BlockSpec((TILE, F), lambda i, idx: (idx[1], 0)),
        pl.BlockSpec((PB, F), lambda i, idx: (idx[2], 0)),
        whole((1, F)),
        pl.BlockSpec((CHUNK, F), lambda i, idx: (i, 0)),
        pl.BlockSpec((1, CHUNK // 128, 128), lambda i, idx: (i, 0, 0)),
    ]
    args = [idx, inducing, inducing, inducing, weights[None, :], x, y.reshape(-1, CHUNK // 128, 128)]
    if not first:
        in_specs += [whole(s) for s in shapes]
        args += list(carry)
    return pl.pallas_call(
        functools.partial(gram_kernel, first),
        grid_spec=pltpu.PrefetchScalarGridSpec(
            num_scalar_prefetch=1,
            grid=(x.shape[0] // CHUNK,),
            in_specs=in_specs,
            out_specs=[whole(s) for s in shapes],
            scratch_shapes=[pltpu.VMEM((2 * TILE + PB, 512), BF16), pltpu.VMEM((CHUNK, 512), BF16)],
        ),
        out_shape=[jax.ShapeDtypeStruct(s, F32) for s in shapes],
        compiler_params=pltpu.CompilerParams(vmem_limit_bytes=48 * 1024 * 1024),
        name="gram_part",
    )(*args)


def factor_kernel(scale_ref, prec_ref, gram_ref, low_ref, inv_ref, work):
    row_id = lax.broadcasted_iota(jnp.int32, (PB, PB), 0)
    col_id = lax.broadcasted_iota(jnp.int32, (PB, PB), 1)
    work[:, 0:PB] = RATE * prec_ref[...] + scale_ref[0] * gram_ref[...]
    work[:, PB:] = jnp.where(row_id == col_id, 1.0, 0.0)
    sub = lax.broadcasted_iota(jnp.int32, (8, 2 * PB), 0)
    lane = lax.broadcasted_iota(jnp.int32, (8, 2 * PB), 1)

    def block(b, _):
        base = pl.multiple_of(8 * b, 8)
        blk = work[pl.ds(base, 8), :]
        for j in range(8):
            at = base + j
            col = jnp.sum(jnp.where(lane == at, blk, 0.0), axis=1, keepdims=True)
            piv = col[j : j + 1, :]
            row = blk[j : j + 1, :] * lax.rsqrt(piv)
            coef = col * lax.rsqrt(piv)
            blk = jnp.where(sub == j, row, jnp.where(sub > j, blk - coef * row, blk))
        work[pl.ds(base, 8), :] = blk
        cols = blk[:, 0:PB].T

        trail = work[...]
        for j in range(8):
            trail = trail - jnp.where(row_id[:, 0:1] >= base + 8, cols[:, j : j + 1], 0.0) * blk[j : j + 1, :]
        work[...] = trail
        return 0

    lax.fori_loop(0, PB // 8, block, 0)
    low_ref[...] = jnp.where(row_id >= col_id, work[:, 0:PB].T, 0.0)
    inv_ref[...] = jnp.where(row_id >= col_id, work[:, PB:], 0.0)


def factored(scale, prec_block, gram_block):
    shape = jax.ShapeDtypeStruct((PB, PB), F32)
    vmem = pl.BlockSpec(memory_space=pltpu.VMEM)
    return pl.pallas_call(
        factor_kernel,
        in_specs=[pl.BlockSpec(memory_space=pltpu.SMEM), vmem, vmem],
        out_specs=[vmem, vmem],
        out_shape=[shape, shape],
        scratch_shapes=[pltpu.VMEM((PB, 2 * PB), F32)],
        name="factored",
    )(scale.reshape(1), prec_block, gram_block)


def local(pool, targets, picks, inducing, inv_sq_lengths, prec_old, mean_old, panel):
    my_row = lax.axis_index(ROW)
    my_col = lax.axis_index(COL)
    my_z = lax.axis_index("z")
    my_core = lax.axis_index("core")
    my_yl = lax.axis_index("yl")
    start = panel[0] * PB
    owner = start // TILE
    offset = start - owner * TILE
    half = offset // PB
    o_yh, o_x, o_core = owner // 8, (owner // 2) % 4, owner % 2
    o_yl, o_z = owner // 8, owner % 8
    o_xy = (o_yh * 4 + o_x) * 2 + o_yl
    zero = jnp.zeros((), jnp.int32)

    samples = jnp.take(pool, picks, axis=0, mode="clip")
    lanes = jnp.arange(128, dtype=jnp.int32)
    own_y = jnp.take(targets, jnp.tile(picks, 8), mode="clip")
    y_row = jnp.where(lanes // 16 == my_z, own_y, jnp.zeros((), BF16))
    columns = lax.dynamic_slice(prec_old, (zero, offset), (TILE, PB))
    chunks = packed(columns.reshape(2, 8, 32, PB).transpose(1, 0, 2, 3).reshape(8, 64, PB))
    common = jnp.concatenate([samples, jnp.pad(y_row[None, :], ((0, 15), (0, 0)))], axis=0)
    z_out = jnp.concatenate([chunks, jnp.broadcast_to(common[None], (8, 32, 128))], axis=1)
    z_in = lax.all_to_all(z_out, "z", 0, 0, tiled=True)
    chunk_q = lax.dynamic_index_in_dim(z_in[:, :256], o_z, 0, keepdims=False)
    z_samples = z_in[:, 256:272].reshape(128, 128)
    z_y = jnp.sum(z_in[:, 272].astype(F32), axis=0).astype(BF16)

    chunk = unpacked(chunk_q)
    chunk = jnp.where(my_yl == o_yl, chunk, swapped(chunk, "yl", 2, 1))

    trace_own = own_trace(inducing, inv_sq_lengths, samples)
    mean_part = lax.dynamic_slice(mean_old, (offset,), (PB,)).reshape(2, 128)
    m_high, m_low = split2(mean_part)
    t_row = jnp.where(lanes == 0, split3(trace_own)[0], jnp.where(lanes == 1, split3(trace_own)[1], jnp.where(lanes == 2, split3(trace_own)[2], jnp.zeros((), BF16))))
    aux = jnp.concatenate([z_y[None], m_high, m_low, t_row[None], jnp.zeros((10, 128), BF16)], axis=0)
    diag_q = lax.dynamic_slice(chunk_q.reshape(4, 2, 32, 128), (zero, half, zero, zero), (4, 1, 32, 128))
    xy_out = jnp.concatenate([z_samples, aux, diag_q.reshape(128, 128)], axis=0)
    xy_in = lax.all_to_all(jnp.broadcast_to(xy_out[None], (16, 272, 128)), XY, 0, 0, tiled=True)
    own_x = xy_in[:, :128].reshape(HALF, 128)
    own_yy = xy_in[:, 128]
    chosen = lax.dynamic_index_in_dim(xy_in, o_xy, 0, keepdims=False)
    diag_mine = chosen[144:272]
    mean_mine = chosen[129:133]
    trace_xy = jnp.sum(xy_in[:, 133, 0:3].astype(F32))

    t1, t2, t3 = split3(trace_xy)
    t_row = jnp.where(lanes == 0, t1, jnp.where(lanes == 1, t2, jnp.where(lanes == 2, t3, jnp.zeros((), BF16))))
    core_out = jnp.concatenate(
        [own_x, own_yy, diag_mine, mean_mine, t_row[None], jnp.zeros((11, 128), BF16)], axis=0
    )
    core_in = swapped(core_out, "core", 2, 1)
    is_owner_core = my_core == o_core
    other_x = core_in[:HALF]
    other_yy = core_in[HALF : HALF + 16]
    tail = jnp.where(is_owner_core, core_out[HALF + 16 :], core_in[HALF + 16 :])
    diag_piece = unpacked(tail[:128])
    mean_panel = (tail[128:130].astype(F32) + tail[130:132].astype(F32)).reshape(PB)
    trace_chip = trace_xy + jnp.sum(core_in[HALF + 16 + 132, 0:3].astype(F32))

    mine = jnp.concatenate([diag_piece, jnp.full((8, PB), trace_chip, F32)], axis=0)
    for k, bit in enumerate((4, 2, 1)):
        mine = joined_along(mine, "z", 8, bit, k)
    mine = mine.reshape(8, 40, PB)
    prec_block = mine[:, :32].reshape(PB, PB)
    trace_scale = jnp.sum(mine[:, 32, 0]) / M

    crossed = lax.ppermute(chunk, ALL, [(16 * i + j, 16 * j + i) for i in range(16) for j in range(16)])
    got_r = chunk
    for k, bit in enumerate((1, 2, 4)):
        got_r = joined_along(got_r, "z", 8, bit, 0)
    got_r = rows_in_order(got_r.reshape(8, 64, PB))
    got_c = joined_along(crossed, "x", 4, 2, 0)
    got_c = joined_along(got_c, "x", 4, 1, 1)
    got_c = joined_along(got_c, "core", 2, 1, 2)
    got_c = rows_in_order(got_c.reshape(8, 64, PB))

    idx = jnp.stack([my_row, my_col, panel[0]]).astype(jnp.int32)
    carry = gram_part(idx, inducing, inv_sq_lengths, own_x, own_yy, None)
    gram, gram_p, fit = gram_part(idx, inducing, inv_sq_lengths, other_x, other_yy, carry)
    fit = jnp.sum(fit, axis=1)
    all_y = jnp.concatenate([own_yy, other_yy], axis=0).astype(F32)
    power_sum = jnp.sum(all_y * all_y)

    scale = RATE / trace_scale
    mean_scale = RATE / jnp.sqrt(trace_scale * (power_sum / B_TOTAL + EPSILON))
    factor, inv_factor = factored(scale, prec_block, gram_p[2 * TILE :])
    joined = RATE * prec_old + scale * gram
    joined_r = RATE * got_r + scale * gram_p[:TILE]
    joined_c = RATE * got_c + scale * gram_p[TILE : 2 * TILE]
    mean_mid = RATE * mean_old + mean_scale * fit[:TILE]
    mean_p = RATE * mean_panel + mean_scale * fit[TILE:]
    wide_r = lax.dot_general(joined_r, inv_factor, NT, precision=HIGHEST)
    wide_ct = lax.dot_general(inv_factor, joined_c, NT, precision=HIGHEST)
    head = jnp.sum(inv_factor * mean_p[None, :], axis=1)
    updated = joined - jnp.dot(wide_r, wide_ct, precision=HIGHEST)
    in_col = my_col == owner
    in_row = my_row == owner
    updated = jnp.where(in_col, lax.dynamic_update_slice(updated, wide_r, (zero, offset)), updated)
    updated = jnp.where(in_row, lax.dynamic_update_slice(updated, wide_ct, (offset, zero)), updated)
    updated = jnp.where(
        jnp.logical_and(in_row, in_col), lax.dynamic_update_slice(updated, factor, (offset, offset)), updated
    )
    mean_next = mean_mid - jnp.sum(wide_r * head[None, :], axis=1)
    mean_next = jnp.where(in_row, lax.dynamic_update_slice(mean_next, head, (offset,)), mean_next)
    return (updated, mean_next)


def solution(mesh):
    split = Mesh(mesh.devices.reshape(2, 4, 2, 2, 8), ALL)
    return jax.shard_map(
        local,
        mesh=split,
        in_specs=(P(ALL, None), P(ALL), P(ALL), P(), P(), P(ROW, COL), P(ROW), P()),
        out_specs=(P(ROW, COL), P(ROW)),
        check_vma=False,
    )
```

```python
import functools
import math

import jax
import jax.numpy as jnp
from jax import lax
from jax.experimental import pallas as pl
from jax.experimental.pallas import tpu as pltpu
from jax.sharding import Mesh
from jax.sharding import PartitionSpec as P

M = 8192
F = 128
PB = 256
TILE = 512
B_TOTAL = 4096
HALF = 2048
CHUNK = 512
ROW = ("yh", "x", "core")
COL = ("yl", "z")
XY = ("yh", "x", "yl")
ALL = ROW + COL
RATE = 0.5
EPSILON = 1e-05
LOG2E = math.log2(math.e)
F32 = jnp.float32
BF16 = jnp.bfloat16
NT = (((1,), (1,)), ((), ()))
HIGHEST = lax.Precision.HIGHEST


def swapped(value, axis, size, bit):
    return lax.ppermute(value, axis, [(i, i ^ bit) for i in range(size)])


def split2(value):
    high = lax.reduce_precision(value, 8, 7)
    return high.astype(BF16), (value - high).astype(BF16)


def split3(value):
    high = lax.reduce_precision(value, 8, 7)
    rest = value - high
    mid = lax.reduce_precision(rest, 8, 7)
    return high.astype(BF16), mid.astype(BF16), (rest - mid).astype(BF16)


def pieces(value):
    high = value.astype(BF16)
    rest = value - high.astype(F32)
    mid = rest.astype(BF16)
    return high, mid, (rest - mid.astype(F32)).astype(BF16)


def scaled_points(pts, w):
    scaled = pts * w * LOG2E
    high = scaled.astype(BF16)
    low = (scaled - high.astype(F32)).astype(BF16)
    return high, low, jnp.sum(pts * pts * w, axis=1, keepdims=True) * (-0.5 * LOG2E)


def sample_terms(x, w):
    xf = x.astype(F32)
    return jnp.sum((xf * xf * w).T, axis=0, keepdims=True) * (-0.5 * LOG2E)


def split_rows(out, at, n, value):
    high = value.astype(BF16)
    low = (value - high.astype(F32)).astype(BF16)
    for k, part in enumerate((high[:, :128], high[:, 128:], low[:, :128], low[:, 128:])):
        out[at + k * n : at + (k + 1) * n, :] = part


def pack_kernel(idx_ref, picks_ref, pool_ref, targets_ref, prec_ref, out_ref):
    sub = lax.broadcasted_iota(jnp.int32, (16, 128), 0)
    lane = lax.broadcasted_iota(jnp.int32, (16, 128), 1)
    at = jnp.zeros((16, 128), jnp.int32)
    for n in range(16):
        at = jnp.where(sub == n, picks_ref[n], at)
    hot = jnp.where(at == lane, 1.0, 0.0)
    samples = jnp.dot(hot.astype(BF16), pool_ref[...], preferred_element_type=F32).astype(BF16)
    y = jnp.sum(hot * targets_ref[...].astype(F32), axis=1, keepdims=True)
    y_row = jnp.sum(jnp.where(lane == 16 * idx_ref[1] + sub, y, 0.0), axis=0, keepdims=True)
    y_rows = jnp.where(sub == 0, y_row, 0.0).astype(BF16)
    for j in range(8):
        chunk = jnp.concatenate([prec_ref[32 * j : 32 * j + 32, :], prec_ref[PB + 32 * j : PB + 32 * j + 32, :]], axis=0)
        split_rows(out_ref.at[j], 0, 64, chunk)
        out_ref[j, 256:272, :] = samples
        out_ref[j, 272:288, :] = y_rows


def pack(idx, picks, pool, targets, prec_old):
    return pl.pallas_call(
        pack_kernel,
        grid_spec=pltpu.PrefetchScalarGridSpec(
            num_scalar_prefetch=2,
            grid=(1,),
            in_specs=[
                pl.BlockSpec((128, 128), lambda i, idx, picks: (0, 0)),
                pl.BlockSpec((1, 128), lambda i, idx, picks: (0, 0)),
                pl.BlockSpec((TILE, PB), lambda i, idx, picks: (0, idx[0])),
            ],
            out_specs=pl.BlockSpec((8, 288, 128), lambda i, idx, picks: (0, 0, 0)),
        ),
        out_shape=jax.ShapeDtypeStruct((8, 288, 128), BF16),
        name="pack",
    )(idx, picks, pool, targets[None, :], prec_old)


def trace_kernel(ind_ref, w_ref, x_ref, out_ref, paug, xaug, total):
    step = pl.program_id(0)
    w = w_ref[...]
    x = x_ref[0]

    @pl.when(step == 0)
    def _():
        total[...] = jnp.zeros_like(total)
        xaug[:, 0:128] = x
        xaug[:, 128:256] = x

    high, low, own = scaled_points(ind_ref[...], w)
    paug[:, 0:128] = high
    paug[:, 128:256] = low
    e = lax.dot_general(paug[...], xaug[...], NT, preferred_element_type=F32)
    f = jnp.exp2(e + own + sample_terms(x, w)).astype(BF16).astype(F32)
    total[:, 0:16] += jnp.sum((f * f).reshape(128, 8, 16), axis=0)

    @pl.when(step == pl.num_programs(0) - 1)
    def _():
        sub = lax.broadcasted_iota(jnp.int32, (16, 128), 0)
        h, m, l = (p.astype(F32) for p in pieces(jnp.sum(total[...], axis=0, keepdims=True)))
        out_ref[...] = jnp.where(sub == 0, h, jnp.where(sub == 1, m, jnp.where(sub == 2, l, 0.0))).astype(BF16)


def trace_rows(inducing, weights, packed):
    return pl.pallas_call(
        trace_kernel,
        grid=(M // 1024,),
        in_specs=[
            pl.BlockSpec((1024, F), lambda i: (i, 0)),
            pl.BlockSpec((1, F), lambda i: (0, 0)),
            pl.BlockSpec((1, 16, F), lambda i: (0, 16, 0)),
        ],
        out_specs=pl.BlockSpec((16, 128), lambda i: (0, 0)),
        out_shape=jax.ShapeDtypeStruct((16, 128), BF16),
        scratch_shapes=[pltpu.VMEM((1024, 256), BF16), pltpu.VMEM((16, 256), BF16), pltpu.VMEM((8, 128), F32)],
        cost_estimate=pl.CostEstimate(flops=4_000_000_000, bytes_accessed=4_000_000, transcendentals=1_000_000),
        name="trace_rows",
    )(inducing, weights[None, :], packed)


def relay_kernel(idx_ref, z_ref, t_ref, mean_ref, out_ref, chunk_ref):
    src, half = idx_ref[0], idx_ref[1]
    sub = lax.broadcasted_iota(jnp.int32, (16, 128), 0)
    chunk = z_ref[src, 0:256, :]
    values = chunk.astype(F32)
    chunk_ref[:, 0:128] = values[0:64] + values[128:192]
    chunk_ref[:, 128:256] = values[64:128] + values[192:256]
    y = jnp.sum(z_ref[:, 272:288, :].astype(F32), axis=0)
    means = mean_ref[pl.ds(2 * half, 2), :]
    m_high = means.astype(BF16).astype(F32)
    m_low = means - m_high
    t = t_ref[...].astype(F32)
    aux = jnp.where(sub == 0, y, 0.0)
    for k, row in enumerate((m_high[0:1], m_high[1:2], m_low[0:1], m_low[1:2], t[0:1], t[1:2], t[2:3])):
        aux = jnp.where(sub == k + 1, row, aux)
    aux = aux.astype(BF16)
    for k in range(4):
        @pl.when(half == 0)
        def _():
            out_ref[0, 144 + 32 * k : 176 + 32 * k, :] = chunk[64 * k : 64 * k + 32]

        @pl.when(half == 1)
        def _():
            out_ref[0, 144 + 32 * k : 176 + 32 * k, :] = chunk[64 * k + 32 : 64 * k + 64]

    out_ref[0, 0:128, :] = z_ref[:, 256:272, :].reshape(128, 128)
    out_ref[0, 128:144, :] = aux
    whole = out_ref[0]
    for k in range(1, 16):
        out_ref[k] = whole


def relay(idx, z_in, t_rows, mean_old):
    vmem = pl.BlockSpec(memory_space=pltpu.VMEM)
    return pl.pallas_call(
        relay_kernel,
        in_specs=[pl.BlockSpec(memory_space=pltpu.SMEM), vmem, vmem, vmem],
        out_specs=[vmem, vmem],
        out_shape=[jax.ShapeDtypeStruct((16, 272, 128), BF16), jax.ShapeDtypeStruct((64, PB), F32)],
        name="relay",
    )(idx, z_in, t_rows, mean_old.reshape(4, 128))


def gram_kernel(first, idx_ref, pr_ref, pc_ref, pp_ref, w_ref, x_ref, y_ref, *refs):
    if first:
        grc_ref, gp_ref, fit_ref, paug, own, xaug = refs
    else:
        grc_in, gp_in, fit_in, grc_ref, gp_ref, fit_ref, paug, own, xaug = refs
    step = pl.program_id(0)

    @pl.when(step == 0)
    def _():
        at = 0
        for ref in (pr_ref, pc_ref, pp_ref):
            n = ref.shape[0]
            high, low, term = scaled_points(ref[...], w_ref[...])
            paug[at : at + n, 0:128] = high
            paug[at : at + n, 128:256] = low
            own[at : at + n, :] = jnp.broadcast_to(term, (n, 128))
            at += n
        if first:
            grc_ref[...] = jnp.zeros_like(grc_ref)
            gp_ref[...] = jnp.zeros_like(gp_ref)
            fit_ref[...] = jnp.zeros_like(fit_ref)
        else:
            grc_ref[...] = grc_in[...]
            gp_ref[...] = gp_in[...]
            fit_ref[...] = fit_in[...]

    x = x_ref[...]
    xaug[:, 0:128] = x
    xaug[:, 128:256] = x
    xa = xaug[...]
    sample_term = sample_terms(x, w_ref[...])

    def feats(at, n):
        e = lax.dot_general(paug[at : at + n, :], xa, NT, preferred_element_type=F32)
        term = own[at : at + n, :]
        e = e + jnp.concatenate([term] * (CHUNK // 128), axis=1) + sample_term
        return jnp.exp2(e).astype(BF16)

    f_r = feats(0, TILE)
    f_c = feats(TILE, TILE)
    f_p = feats(2 * TILE, PB)
    grc_ref[...] += lax.dot_general(f_r, f_c, NT, preferred_element_type=F32)
    gp_ref[0:TILE, :] += lax.dot_general(f_r, f_p, NT, preferred_element_type=F32)
    gp_ref[TILE : 2 * TILE, :] += lax.dot_general(f_c, f_p, NT, preferred_element_type=F32)
    gp_ref[2 * TILE :, :] += lax.dot_general(f_p, f_p, NT, preferred_element_type=F32)
    y = y_ref[...].reshape(CHUNK // 128, 128).astype(F32)
    for at, f in ((0, f_r), (TILE, f_p)):
        acc = fit_ref[at : at + f.shape[0], :]
        for k in range(CHUNK // 128):
            acc = acc + f[:, 128 * k : 128 * (k + 1)].astype(F32) * y[k : k + 1, :]
        fit_ref[at : at + f.shape[0], :] = acc


def gram_part(idx, inducing, weights, x, y, carry):
    first = carry is None
    whole = lambda shape: pl.BlockSpec(shape, lambda i, idx: (0,) * len(shape))
    shapes = ((TILE, TILE), (2 * TILE + PB, PB), (TILE + PB, 128))
    in_specs = [
        pl.BlockSpec((TILE, F), lambda i, idx: (idx[0], 0)),
        pl.BlockSpec((TILE, F), lambda i, idx: (idx[1], 0)),
        pl.BlockSpec((PB, F), lambda i, idx: (idx[2], 0)),
        whole((1, F)),
        pl.BlockSpec((CHUNK, F), lambda i, idx: (i, 0)),
        pl.BlockSpec((1, CHUNK // 128, 128), lambda i, idx: (i, 0, 0)),
    ]
    args = [idx, inducing, inducing, inducing, weights[None, :], x, y.reshape(-1, CHUNK // 128, 128)]
    if not first:
        in_specs += [whole(s) for s in shapes]
        args += list(carry)
    return pl.pallas_call(
        functools.partial(gram_kernel, first),
        grid_spec=pltpu.PrefetchScalarGridSpec(
            num_scalar_prefetch=1,
            grid=(x.shape[0] // CHUNK,),
            in_specs=in_specs,
            out_specs=[whole(s) for s in shapes],
            scratch_shapes=[
                pltpu.VMEM((2 * TILE + PB, 256), BF16),
                pltpu.VMEM((2 * TILE + PB, 128), F32),
                pltpu.VMEM((CHUNK, 256), BF16),
            ],
        ),
        out_shape=[jax.ShapeDtypeStruct(s, F32) for s in shapes],
        compiler_params=pltpu.CompilerParams(vmem_limit_bytes=48 * 1024 * 1024),
        cost_estimate=pl.CostEstimate(flops=12_000_000_000, bytes_accessed=8_000_000, transcendentals=2_600_000),
        name="gram_part",
    )(*args)


def trace_scale_of(diag_ref):
    traces = jnp.zeros((1, 128), F32)
    for j in range(8):
        traces = traces + (diag_ref[j, 32:33, 0:128] + diag_ref[j, 33:34, 0:128])
    return jnp.sum(traces, axis=1, keepdims=True) * (1.0 / M)


def factor_kernel(diag_ref, gp_ref, low_ref, inv_ref, work, cols, dinv, mrow):
    row_id = lax.broadcasted_iota(jnp.int32, (PB, PB), 0)
    col_id = lax.broadcasted_iota(jnp.int32, (PB, PB), 1)
    scale = trace_scale_of(diag_ref)
    scale = RATE / scale
    for j in range(8):
        rows = slice(32 * j, 32 * j + 32)
        work[rows, 0:PB] = RATE * diag_ref[j, 0:32, :] + scale * gp_ref[2 * TILE + 32 * j : 2 * TILE + 32 * j + 32, :]
    work[:, PB:] = jnp.where(row_id == col_id, 1.0, 0.0)
    for b in range(PB // 8):
        base = 8 * b
        tile = base // 128 * 128
        spans = [t for t in range(0, 2 * PB, 128) if (tile <= t < PB) or PB <= t <= PB + base]
        d8 = work[base : base + 8, tile : tile + 128]
        for k in range(8):
            cols[8 * k : 8 * k + 8, :] = jnp.broadcast_to(d8[:, base - tile + k : base - tile + k + 1], (8, 128))
        d = {(i, k): cols[8 * k + i : 8 * k + i + 1, :] for k in range(8) for i in range(k, 8)}
        low = {}
        rs = {}
        m = {}
        for k in range(8):
            rs[k] = lax.rsqrt(d[k, k])
            for i in range(k + 1, 8):
                low[i, k] = d[i, k] * rs[k]
            for i in range(k + 1, 8):
                for j in range(k + 1, i + 1):
                    d[i, j] = d[i, j] - low[i, k] * low[j, k]
            m[k, k] = rs[k]
            for j in range(k):
                acc = low[k, j] * m[j, j]
                for t in range(j + 1, k):
                    acc = acc + low[k, t] * m[t, j]
                m[k, j] = -acc * rs[k]
        zero = jnp.zeros((1, 128), F32)
        for j in range(8):
            for i in range(8):
                mrow[8 * j + i : 8 * j + i + 1, :] = m[i, j] if i >= j else zero
        for i in range(8):
            for j in range(i, 8):
                acc = m[j, i] * m[j, j]
                for t in range(j + 1, 8):
                    acc = acc + m[t, i] * m[t, j]
                dinv[8 * j + i : 8 * j + i + 1, :] = acc
                if i != j:
                    dinv[8 * i + j : 8 * i + j + 1, :] = acc
        t_rows = {}
        for s in spans:
            u = None
            tt = None
            for j in range(8):
                r = work[base + j : base + j + 1, s : s + 128]
                if b + 1 < PB // 8:
                    q = dinv[8 * j : 8 * j + 8, :] * r
                    tt = q if tt is None else tt + q
                q = mrow[8 * j : 8 * j + 8, :] * r
                u = q if u is None else u + q
            t_rows[s] = tt
            work[base : base + 8, s : s + 128] = u
        for s in spans:
            if t_rows[s] is not None:
                cols[64 + 8 * (s // 128) : 72 + 8 * (s // 128), :] = t_rows[s]
        for g in range(b + 1, PB // 8):
            rows = slice(8 * g, 8 * g + 8)
            a = work[rows, tile : tile + 128]
            coef = [jnp.broadcast_to(a[:, base - tile + k : base - tile + k + 1], (8, 128)) for k in range(8)]
            for s in spans:
                v = work[rows, s : s + 128]
                for k in range(8):
                    v = v - coef[k] * cols[64 + 8 * (s // 128) + k : 65 + 8 * (s // 128) + k, :]
                work[rows, s : s + 128] = v
    low_ref[...] = jnp.where(row_id >= col_id, work[:, 0:PB].T, 0.0)
    inv_ref[...] = jnp.where(row_id >= col_id, work[:, PB:], 0.0)


def factored(diag, gram_p):
    vmem = pl.BlockSpec(memory_space=pltpu.VMEM)
    shape = jax.ShapeDtypeStruct((PB, PB), F32)
    return pl.pallas_call(
        factor_kernel,
        in_specs=[vmem, vmem],
        out_specs=[vmem, vmem],
        out_shape=[shape, shape],
        scratch_shapes=[
            pltpu.VMEM((PB, 2 * PB), F32),
            pltpu.VMEM((96, 128), F32),
            pltpu.VMEM((64, 128), F32),
            pltpu.VMEM((64, 128), F32),
        ],
        cost_estimate=pl.CostEstimate(flops=16_000_000_000, bytes_accessed=1_000_000, transcendentals=1000),
        name="factored",
    )(diag, gram_p)


def finish_kernel(
    idx_ref, diag_ref, y_ref, mo_ref, low_ref, inv_ref, gram_ref, gp_ref, fit_ref, gr_ref, gc_ref, prec_ref,
    out_ref, mean_ref, jr, jc,
):
    my_z, my_xc, half, in_row, in_col = (idx_ref[k] for k in range(5))
    trace_scale = trace_scale_of(diag_ref)
    scale = RATE / trace_scale
    ys = y_ref[...].astype(F32)
    power = jnp.sum(jnp.sum(ys * ys, axis=0, keepdims=True), axis=1, keepdims=True)
    mean_scale = RATE / jnp.sqrt(trace_scale * (power * (1.0 / B_TOTAL) + EPSILON))
    inv = inv_ref[...]
    for j in range(8):
        for h in range(2):
            at = h * PB + 32 * j
            rows = slice(at, at + 32)
            part = slice(32 * h, 32 * h + 32)
            jr[rows, :] = RATE * gr_ref[j ^ my_z, part, :] + scale * gp_ref[rows, :]
            jc[rows, :] = RATE * gc_ref[j ^ my_xc, part, :] + scale * gp_ref[TILE + at : TILE + at + 32, :]
    wide_r = lax.dot_general(jr[...], inv, NT, precision=HIGHEST, preferred_element_type=F32)
    wide_ct = lax.dot_general(inv, jc[...], NT, precision=HIGHEST, preferred_element_type=F32)
    taken = jnp.dot(wide_r, wide_ct, precision=HIGHEST, preferred_element_type=F32)
    out_ref[...] = RATE * prec_ref[...] + scale * gram_ref[...] - taken
    mean_p = RATE * diag_ref[0, 34:35, :] + mean_scale * jnp.sum(fit_ref[TILE:, :].T, axis=0, keepdims=True)
    mean_mid = RATE * mo_ref[...] + mean_scale * jnp.sum(fit_ref[0:TILE, :].T, axis=0, keepdims=True)
    head = lax.dot_general(mean_p, inv, NT, precision=HIGHEST, preferred_element_type=F32)
    mean_ref[...] = mean_mid - lax.dot_general(head, wide_r, NT, precision=HIGHEST, preferred_element_type=F32)
    for h in range(2):
        span = slice(h * PB, h * PB + PB)

        @pl.when((in_col == 1) & (half == h))
        def _():
            out_ref[:, span] = wide_r

        @pl.when((in_row == 1) & (half == h))
        def _():
            out_ref[span, :] = wide_ct
            mean_ref[:, span] = head

        @pl.when((in_row == 1) & (in_col == 1) & (half == h))
        def _():
            out_ref[span, span] = low_ref[...]


def finish(idx, *args):
    vmem = pl.BlockSpec(memory_space=pltpu.VMEM)
    return pl.pallas_call(
        finish_kernel,
        in_specs=[pl.BlockSpec(memory_space=pltpu.SMEM)] + [vmem] * len(args),
        out_specs=[vmem, vmem],
        out_shape=[jax.ShapeDtypeStruct((TILE, TILE), F32), jax.ShapeDtypeStruct((1, TILE), F32)],
        scratch_shapes=[pltpu.VMEM((TILE, PB), F32), pltpu.VMEM((TILE, PB), F32)],
        compiler_params=pltpu.CompilerParams(vmem_limit_bytes=48 * 1024 * 1024),
        cost_estimate=pl.CostEstimate(flops=4_000_000_000, bytes_accessed=4_000_000, transcendentals=1000),
        name="finish",
    )(idx, *args)


def local(pool, targets, picks, inducing, inv_sq_lengths, prec_old, mean_old, panel):
    my_row = lax.axis_index(ROW)
    my_col = lax.axis_index(COL)
    my_z = lax.axis_index("z")
    my_x = lax.axis_index("x")
    my_core = lax.axis_index("core")
    my_yl = lax.axis_index("yl")
    owner = panel[0] // 2
    half = panel[0] - 2 * owner
    o_yh, o_x, o_core = owner // 8, (owner // 2) % 4, owner % 2
    o_yl, o_z = owner // 8, owner % 8
    o_xy = (o_yh * 4 + o_x) * 2 + o_yl

    def ints(*values):
        lanes = jnp.arange(len(values), dtype=jnp.int32)
        out = jnp.zeros(len(values), jnp.int32)
        for k, v in enumerate(values):
            out = jnp.where(lanes == k, v.astype(jnp.int32), out)
        return out

    z_out = pack(ints(half, my_z), picks, pool, targets, prec_old)
    z_in = lax.all_to_all(z_out, "z", 0, 0, tiled=True)
    t_rows = trace_rows(inducing, inv_sq_lengths, z_out)

    xy_out, chunk = relay(ints(o_z, half), z_in, t_rows, mean_old)
    xy_in = lax.all_to_all(xy_out, XY, 0, 0, tiled=True)
    chunk = jnp.where(my_yl == o_yl, chunk, swapped(chunk, "yl", 2, 1))
    xy_in, chunk = lax.optimization_barrier((xy_in, chunk))

    own_x = xy_in[:, :128].reshape(HALF, 128)
    own_yy = xy_in[:, 128]
    chosen = lax.dynamic_index_in_dim(xy_in, o_xy, 0, keepdims=False).astype(F32)
    trace_xy = jnp.sum(xy_in[:, 133:136].astype(F32), axis=(0, 1))
    diag_piece = jnp.concatenate(
        [chosen[144:176] + chosen[208:240], chosen[176:208] + chosen[240:272]], axis=1
    )
    mean_panel = (chosen[129:131] + chosen[131:133]).reshape(1, PB)
    wide_trace = jnp.pad(trace_xy[None, :], ((0, 0), (0, 128)))
    mine = jnp.concatenate([diag_piece, wide_trace, mean_panel, jnp.zeros((6, PB), F32)], axis=0)
    blocks = lax.all_to_all(jnp.broadcast_to(mine[None], (8, 40, PB)), "z", 0, 0, tiled=True)
    core_in = swapped(jnp.concatenate([own_x, own_yy], axis=0), "core", 2, 1)
    far_r = swapped(chunk, "z", 8, 4)
    crossed = lax.ppermute(chunk, ALL, [(16 * i + j, 16 * j + i) for i in range(16) for j in range(16)])
    idx = ints(my_row, my_col, panel[0])
    carry = gram_part(idx, inducing, inv_sq_lengths, own_x, own_yy, None)
    carry, blocks, core_in, far_r, crossed, chunk, own_yy = lax.optimization_barrier(
        (carry, blocks, core_in, far_r, crossed, chunk, own_yy)
    )

    other_x = core_in[:HALF]
    other_yy = core_in[HALF : HALF + 16]
    blocks_in = swapped(blocks, "core", 2, 1)
    two_r = jnp.stack([chunk, far_r])
    two_r = jnp.stack([two_r, swapped(two_r, "z", 8, 2)], axis=1)
    two_c = jnp.stack([crossed, swapped(crossed, "core", 2, 1)])
    gram, gram_p, fit = gram_part(idx, inducing, inv_sq_lengths, other_x, other_yy, carry)
    here = my_core == o_core
    diag = jnp.concatenate(
        [
            jnp.where(here, blocks[:, :32], blocks_in[:, :32]),
            blocks[:, 32:33],
            blocks_in[:, 32:33],
            jnp.where(here, blocks[:, 33:34], blocks_in[:, 33:34]),
            jnp.zeros((8, 5, PB), F32),
        ],
        axis=1,
    )
    gram, gram_p, fit, diag, two_r, two_c = lax.optimization_barrier((gram, gram_p, fit, diag, two_r, two_c))

    got_r = jnp.stack([two_r, swapped(two_r, "z", 8, 1)], axis=2)
    got_c = jnp.stack([two_c] + [swapped(two_c, "x", 4, k) for k in (1, 2, 3)])
    factor, inv_factor = factored(diag, gram_p)
    all_y = jnp.concatenate([own_yy, other_yy], axis=0)
    in_row = my_row == owner
    in_col = my_col == owner
    updated, mean_next = finish(
        ints(my_z, 2 * my_x + my_core, half, in_row, in_col),
        diag,
        all_y,
        mean_old.reshape(1, TILE),
        factor,
        inv_factor,
        gram,
        gram_p,
        fit,
        got_r.reshape(8, 64, PB),
        got_c.reshape(8, 64, PB),
        prec_old,
    )
    return (updated, mean_next.reshape(TILE))


def solution(mesh):
    split = Mesh(mesh.devices.reshape(2, 4, 2, 2, 8), ALL)
    return jax.shard_map(
        local,
        mesh=split,
        in_specs=(P(ALL, None), P(ALL), P(ALL), P(), P(), P(ROW, COL), P(ROW), P()),
        out_specs=(P(ROW, COL), P(ROW)),
        check_vma=False,
    )
```

```python
import functools
import math

import jax
import jax.numpy as jnp
from jax import lax
from jax.experimental import pallas as pl
from jax.experimental.pallas import tpu as pltpu
from jax.sharding import Mesh
from jax.sharding import PartitionSpec as P

M = 8192
F = 128
PB = 256
TILE = 512
B_TOTAL = 4096
HALF = 2048
CHUNK = 512
ROW = ("yh", "x", "core")
COL = ("yl", "z")
XY = ("yh", "x", "yl")
ALL = ROW + COL
RATE = 0.5
EPSILON = 1e-05
LOG2E = math.log2(math.e)
F32 = jnp.float32
BF16 = jnp.bfloat16
NT = (((1,), (1,)), ((), ()))
HIGHEST = lax.Precision.HIGHEST


def swapped(value, axis, size, bit):
    return lax.ppermute(value, axis, [(i, i ^ bit) for i in range(size)])


def split2(value):
    high = lax.reduce_precision(value, 8, 7)
    return high.astype(BF16), (value - high).astype(BF16)


def split3(value):
    high = lax.reduce_precision(value, 8, 7)
    rest = value - high
    mid = lax.reduce_precision(rest, 8, 7)
    return high.astype(BF16), mid.astype(BF16), (rest - mid).astype(BF16)


def pieces(value):
    high = value.astype(BF16)
    rest = value - high.astype(F32)
    mid = rest.astype(BF16)
    return high, mid, (rest - mid.astype(F32)).astype(BF16)


def scaled_points(pts, w):
    scaled = pts * w * LOG2E
    high = scaled.astype(BF16)
    low = (scaled - high.astype(F32)).astype(BF16)
    return high, low, jnp.sum(pts * pts * w, axis=1, keepdims=True) * (-0.5 * LOG2E)


def sample_terms(x, w):
    xf = x.astype(F32)
    return jnp.sum((xf * xf * w).T, axis=0, keepdims=True) * (-0.5 * LOG2E)


def split_rows(out, at, n, value):
    high = value.astype(BF16)
    low = (value - high.astype(F32)).astype(BF16)
    for k, part in enumerate((high[:, :128], high[:, 128:], low[:, :128], low[:, 128:])):
        out[at + k * n : at + (k + 1) * n, :] = part


def pack_kernel(idx_ref, picks_ref, pool_ref, targets_ref, prec_ref, out_ref):
    sub = lax.broadcasted_iota(jnp.int32, (16, 128), 0)
    lane = lax.broadcasted_iota(jnp.int32, (16, 128), 1)
    at = jnp.zeros((16, 128), jnp.int32)
    for n in range(16):
        at = jnp.where(sub == n, picks_ref[n], at)
    hot = jnp.where(at == lane, 1.0, 0.0)
    samples = jnp.dot(hot.astype(BF16), pool_ref[...], preferred_element_type=F32).astype(BF16)
    y = jnp.sum(hot * targets_ref[...].astype(F32), axis=1, keepdims=True)
    y_row = jnp.sum(jnp.where(lane == 16 * idx_ref[1] + sub, y, 0.0), axis=0, keepdims=True)
    y_rows = jnp.where(sub == 0, y_row, 0.0).astype(BF16)
    for j in range(8):
        chunk = jnp.concatenate([prec_ref[128 * q + 16 * j : 128 * q + 16 * j + 16, :] for q in range(4)], axis=0)
        split_rows(out_ref.at[j], 0, 64, chunk)
        out_ref[j, 256:272, :] = samples
        out_ref[j, 272:288, :] = y_rows


def pack(idx, picks, pool, targets, prec_old):
    return pl.pallas_call(
        pack_kernel,
        grid_spec=pltpu.PrefetchScalarGridSpec(
            num_scalar_prefetch=2,
            grid=(1,),
            in_specs=[
                pl.BlockSpec((128, 128), lambda i, idx, picks: (0, 0)),
                pl.BlockSpec((1, 128), lambda i, idx, picks: (0, 0)),
                pl.BlockSpec((TILE, PB), lambda i, idx, picks: (0, idx[0])),
            ],
            out_specs=pl.BlockSpec((8, 288, 128), lambda i, idx, picks: (0, 0, 0)),
        ),
        out_shape=jax.ShapeDtypeStruct((8, 288, 128), BF16),
        name="pack",
    )(idx, picks, pool, targets[None, :], prec_old)


def trace_kernel(ind_ref, w_ref, x_ref, out_ref, paug, xaug, total):
    step = pl.program_id(0)
    w = w_ref[...]
    x = x_ref[0]

    @pl.when(step == 0)
    def _():
        total[...] = jnp.zeros_like(total)
        xaug[:, 0:128] = x
        xaug[:, 128:256] = x

    high, low, own = scaled_points(ind_ref[...], w)
    paug[:, 0:128] = high
    paug[:, 128:256] = low
    e = lax.dot_general(paug[...], xaug[...], NT, preferred_element_type=F32)
    f = jnp.exp2(e + own + sample_terms(x, w)).astype(BF16).astype(F32)
    total[:, 0:16] += jnp.sum((f * f).reshape(128, 8, 16), axis=0)

    @pl.when(step == pl.num_programs(0) - 1)
    def _():
        sub = lax.broadcasted_iota(jnp.int32, (16, 128), 0)
        h, m, l = (p.astype(F32) for p in pieces(jnp.sum(total[...], axis=0, keepdims=True)))
        out_ref[...] = jnp.where(sub == 0, h, jnp.where(sub == 1, m, jnp.where(sub == 2, l, 0.0))).astype(BF16)


def trace_rows(inducing, weights, packed):
    return pl.pallas_call(
        trace_kernel,
        grid=(M // 1024,),
        in_specs=[
            pl.BlockSpec((1024, F), lambda i: (i, 0)),
            pl.BlockSpec((1, F), lambda i: (0, 0)),
            pl.BlockSpec((1, 16, F), lambda i: (0, 16, 0)),
        ],
        out_specs=pl.BlockSpec((16, 128), lambda i: (0, 0)),
        out_shape=jax.ShapeDtypeStruct((16, 128), BF16),
        scratch_shapes=[pltpu.VMEM((1024, 256), BF16), pltpu.VMEM((16, 256), BF16), pltpu.VMEM((8, 128), F32)],
        cost_estimate=pl.CostEstimate(flops=4_000_000_000, bytes_accessed=4_000_000, transcendentals=1_000_000),
        name="trace_rows",
    )(inducing, weights[None, :], packed)


def relay_kernel(idx_ref, z_ref, t_ref, mean_ref, out_ref, chunk_ref):
    src, half, my_z = idx_ref[0], idx_ref[1], idx_ref[2]
    sub = lax.broadcasted_iota(jnp.int32, (16, 128), 0)
    lane = lax.broadcasted_iota(jnp.int32, (16, 128), 1)
    values = z_ref[src, 0:256, :].astype(F32)
    chunk_ref[:, 0:128] = values[0:64] + values[128:192]
    chunk_ref[:, 128:256] = values[64:128] + values[192:256]
    parts, diagonals = [], []
    for k in range(2):
        left, right = values[128 * k : 128 * k + 64], values[128 * k + 64 : 128 * k + 128]
        top = jnp.where(half == 0, left[0:16], left[32:48])
        low_left = jnp.where(half == 0, left[16:32], left[48:64])
        low_right = jnp.where(half == 0, right[16:32], right[48:64])
        own = 16 * my_z + sub
        parts += [low_left, jnp.where(lane <= own, top, low_right)]
        diagonals.append(jnp.sum(jnp.where(lane == own, low_right, 0.0), axis=0, keepdims=True))
    y = jnp.sum(z_ref[:, 272:288, :].astype(F32), axis=0)
    means = mean_ref[pl.ds(2 * half, 2), :]
    m_high = means.astype(BF16).astype(F32)
    m_low = means - m_high
    t = t_ref[...].astype(F32)
    aux = jnp.where(sub == 0, y, 0.0)
    rows = (m_high[0:1], m_high[1:2], m_low[0:1], m_low[1:2], t[0:1], t[1:2], t[2:3], *diagonals)
    for k, row in enumerate(rows):
        aux = jnp.where(sub == k + 1, row, aux)
    whole = jnp.concatenate([p.astype(BF16) for p in (aux, *parts)], axis=0)
    samples = z_ref[:, 256:272, :].reshape(128, 128)
    for k in range(16):
        out_ref[k, 0:128, :] = samples
        out_ref[k, 128:208, :] = whole


def relay(idx, z_in, t_rows, mean_old):
    vmem = pl.BlockSpec(memory_space=pltpu.VMEM)
    return pl.pallas_call(
        relay_kernel,
        in_specs=[pl.BlockSpec(memory_space=pltpu.SMEM), vmem, vmem, vmem],
        out_specs=[vmem, vmem],
        out_shape=[jax.ShapeDtypeStruct((16, 208, 128), BF16), jax.ShapeDtypeStruct((64, PB), F32)],
        name="relay",
    )(idx, z_in, t_rows, mean_old.reshape(4, 128))


def gram_kernel(idx_ref, pr_ref, pc_ref, pp_ref, w_ref, x_ref, y_ref, grc_ref, gp_ref, fit_ref, paug, own, xaug, ys):
    step = pl.program_id(0)

    @pl.when(step == 0)
    def _():
        at = 0
        for ref in (pr_ref, pc_ref, pp_ref):
            n = ref.shape[0]
            high, low, term = scaled_points(ref[...], w_ref[...])
            paug[at : at + n, 0:128] = high
            paug[at : at + n, 128:256] = low
            own[at : at + n, :] = jnp.broadcast_to(term, (n, 128))
            at += n
        y_all = (y_ref[:, 0, :] if len(y_ref.shape) == 3 else y_ref[...]).astype(F32)
        for k in range(4):
            ys[k, 0:4, :] = y_all[4 * k : 4 * k + 4]
        grc_ref[...] = jnp.zeros_like(grc_ref)
        gp_ref[...] = jnp.zeros_like(gp_ref)
        fit_ref[...] = jnp.zeros_like(fit_ref)
        fit_ref[TILE + PB : TILE + PB + 1, :] = jnp.sum(y_all * y_all, axis=0, keepdims=True)

    x = x_ref[...].reshape(CHUNK, F)
    xaug[:, 0:128] = x
    xaug[:, 128:256] = x
    xa = xaug[...]
    sample_term = sample_terms(x, w_ref[...])

    def feats(at, n):
        e = lax.dot_general(paug[at : at + n, :], xa, NT, preferred_element_type=F32)
        term = own[at : at + n, :]
        e = e + jnp.concatenate([term] * (CHUNK // 128), axis=1) + sample_term
        return jnp.exp2(e).astype(BF16)

    f_r = feats(0, TILE)
    f_c = feats(TILE, TILE)
    f_p = feats(2 * TILE, PB)
    grc_ref[...] += lax.dot_general(f_r, f_c, NT, preferred_element_type=F32)
    gp_ref[0:TILE, :] += lax.dot_general(f_r, f_p, NT, preferred_element_type=F32)
    gp_ref[TILE : 2 * TILE, :] += lax.dot_general(f_c, f_p, NT, preferred_element_type=F32)
    gp_ref[2 * TILE :, :] += lax.dot_general(f_p, f_p, NT, preferred_element_type=F32)
    y = ys[step]
    for at, f in ((0, f_r), (TILE, f_p)):
        acc = fit_ref[at : at + f.shape[0], :]
        for k in range(CHUNK // 128):
            acc = acc + f[:, 128 * k : 128 * (k + 1)].astype(F32) * y[k : k + 1, :]
        fit_ref[at : at + f.shape[0], :] = acc


def gram_part(idx, inducing, weights, source, x_spec, y_spec):
    shapes = ((TILE, TILE), (2 * TILE + PB, PB), (TILE + PB + 8, 128))
    return pl.pallas_call(
        gram_kernel,
        grid_spec=pltpu.PrefetchScalarGridSpec(
            num_scalar_prefetch=1,
            grid=(HALF // CHUNK,),
            in_specs=[
                pl.BlockSpec((TILE, F), lambda i, idx: (idx[0], 0)),
                pl.BlockSpec((TILE, F), lambda i, idx: (idx[1], 0)),
                pl.BlockSpec((PB, F), lambda i, idx: (idx[2], 0)),
                pl.BlockSpec((1, F), lambda i, idx: (0, 0)),
                x_spec,
                y_spec,
            ],
            out_specs=[pl.BlockSpec(s, lambda i, idx: (0, 0)) for s in shapes],
            scratch_shapes=[
                pltpu.VMEM((2 * TILE + PB, 256), BF16),
                pltpu.VMEM((2 * TILE + PB, 128), F32),
                pltpu.VMEM((CHUNK, 256), BF16),
                pltpu.VMEM((4, 8, 128), F32),
            ],
        ),
        out_shape=[jax.ShapeDtypeStruct(s, F32) for s in shapes],
        compiler_params=pltpu.CompilerParams(vmem_limit_bytes=48 * 1024 * 1024),
        cost_estimate=pl.CostEstimate(flops=12_000_000_000, bytes_accessed=8_000_000, transcendentals=2_600_000),
        name="gram_part",
    )(idx, inducing, inducing, inducing, weights[None, :], source, source)


def trace_scale_of(near_ref, far_ref):
    traces = jnp.zeros((1, 128), F32)
    for j in range(8):
        traces = traces + (near_ref[j, 16:17, 0:128] + far_ref[j, 16:17, 0:128])
    return jnp.sum(traces, axis=1, keepdims=True) * (1.0 / M)


def factor_kernel(idx_ref, near_ref, far_ref, gp1_ref, gp2_ref, low_ref, inv_ref, work, cols, dinv, mrow):
    here = idx_ref[0] == 1
    row_id = lax.broadcasted_iota(jnp.int32, (PB, PB), 0)
    col_id = lax.broadcasted_iota(jnp.int32, (PB, PB), 1)
    low = lax.broadcasted_iota(jnp.int32, (128, 128), 0)
    lane = lax.broadcasted_iota(jnp.int32, (128, 128), 1)
    scale = RATE / trace_scale_of(near_ref, far_ref)
    blocks = [jnp.where(here, near_ref[j], far_ref[j]) for j in range(8)]
    both = jnp.concatenate([b[0:16, 0:128] for b in blocks], axis=0)
    low_left = jnp.concatenate([b[0:16, 128:256] for b in blocks], axis=0)
    diagonal = jnp.concatenate([jnp.broadcast_to(b[16:17, 128:256], (16, 128)) for b in blocks], axis=0)
    on = low == lane
    under = jnp.where(low > lane, both, 0.0)
    over = jnp.where(low < lane, both, 0.0)
    gram = scale * (gp1_ref[2 * TILE :, :] + gp2_ref[2 * TILE :, :])
    work[0:128, 0:128] = RATE * (under + under.T + jnp.where(on, both, 0.0)) + gram[0:128, 0:128]
    work[0:128, 128:256] = RATE * low_left.T + gram[0:128, 128:256]
    work[128:256, 0:128] = RATE * low_left + gram[128:256, 0:128]
    work[128:256, 128:256] = RATE * (over + over.T + jnp.where(on, diagonal, 0.0)) + gram[128:256, 128:256]
    work[:, PB:] = jnp.where(row_id == col_id, 1.0, 0.0)
    for b in range(PB // 8):
        base = 8 * b
        tile = base // 128 * 128
        spans = [t for t in range(0, 2 * PB, 128) if (tile <= t < PB) or PB <= t <= PB + base]
        d8 = work[base : base + 8, tile : tile + 128]
        for k in range(8):
            cols[8 * k : 8 * k + 8, :] = jnp.broadcast_to(d8[:, base - tile + k : base - tile + k + 1], (8, 128))
        d = {(i, k): cols[8 * k + i : 8 * k + i + 1, :] for k in range(8) for i in range(k, 8)}
        lo = {}
        rs = {}
        m = {}
        for k in range(8):
            rs[k] = lax.rsqrt(d[k, k])
            for i in range(k + 1, 8):
                lo[i, k] = d[i, k] * rs[k]
            for i in range(k + 1, 8):
                for j in range(k + 1, i + 1):
                    d[i, j] = d[i, j] - lo[i, k] * lo[j, k]
            m[k, k] = rs[k]
            for j in range(k):
                acc = lo[k, j] * m[j, j]
                for t in range(j + 1, k):
                    acc = acc + lo[k, t] * m[t, j]
                m[k, j] = -acc * rs[k]
        zero = jnp.zeros((1, 128), F32)
        for j in range(8):
            for i in range(8):
                mrow[8 * j + i : 8 * j + i + 1, :] = m[i, j] if i >= j else zero
        for i in range(8):
            for j in range(i, 8):
                acc = m[j, i] * m[j, j]
                for t in range(j + 1, 8):
                    acc = acc + m[t, i] * m[t, j]
                dinv[8 * j + i : 8 * j + i + 1, :] = acc
                if i != j:
                    dinv[8 * i + j : 8 * i + j + 1, :] = acc
        t_rows = {}
        for s in spans:
            u = None
            tt = None
            for j in range(8):
                r = work[base + j : base + j + 1, s : s + 128]
                if b + 1 < PB // 8:
                    q = dinv[8 * j : 8 * j + 8, :] * r
                    tt = q if tt is None else tt + q
                q = mrow[8 * j : 8 * j + 8, :] * r
                u = q if u is None else u + q
            t_rows[s] = tt
            work[base : base + 8, s : s + 128] = u
        for s in spans:
            if t_rows[s] is not None:
                cols[64 + 8 * (s // 128) : 72 + 8 * (s // 128), :] = t_rows[s]
        for g in range(b + 1, PB // 8):
            rows = slice(8 * g, 8 * g + 8)
            a = work[rows, tile : tile + 128]
            coef = [jnp.broadcast_to(a[:, base - tile + k : base - tile + k + 1], (8, 128)) for k in range(8)]
            for s in spans:
                v = work[rows, s : s + 128]
                for k in range(8):
                    v = v - coef[k] * cols[64 + 8 * (s // 128) + k : 65 + 8 * (s // 128) + k, :]
                work[rows, s : s + 128] = v
    low_ref[...] = jnp.where(row_id >= col_id, work[:, 0:PB].T, 0.0)
    inv_ref[...] = jnp.where(row_id >= col_id, work[:, PB:], 0.0)


def factored(idx, near, far, gp1, gp2):
    vmem = pl.BlockSpec(memory_space=pltpu.VMEM)
    shape = jax.ShapeDtypeStruct((PB, PB), F32)
    return pl.pallas_call(
        factor_kernel,
        in_specs=[pl.BlockSpec(memory_space=pltpu.SMEM), vmem, vmem, vmem, vmem],
        out_specs=[vmem, vmem],
        out_shape=[shape, shape],
        scratch_shapes=[
            pltpu.VMEM((PB, 2 * PB), F32),
            pltpu.VMEM((96, 128), F32),
            pltpu.VMEM((64, 128), F32),
            pltpu.VMEM((64, 128), F32),
        ],
        cost_estimate=pl.CostEstimate(flops=16_000_000_000, bytes_accessed=1_000_000, transcendentals=1000),
        name="factored",
    )(idx, near, far, gp1, gp2)


def finish_kernel(
    idx_ref, near_ref, far_ref, mo_ref, low_ref, inv_ref, g1_ref, g2_ref, gp1_ref, gp2_ref, fit1_ref, fit2_ref,
    gr_ref, gc_ref, prec_ref, out_ref, mean_ref, jr, jc,
):
    my_z, my_xc, half, in_row, in_col, here = (idx_ref[k] for k in range(6))
    trace_scale = trace_scale_of(near_ref, far_ref)
    scale = RATE / trace_scale
    fit = fit1_ref[...] + fit2_ref[...]
    power = jnp.sum(fit[TILE + PB : TILE + PB + 1, :], axis=1, keepdims=True)
    mean_scale = RATE / jnp.sqrt(trace_scale * (power * (1.0 / B_TOTAL) + EPSILON))
    inv = inv_ref[...]
    for j in range(8):
        for q in range(4):
            rows = slice(128 * q + 16 * j, 128 * q + 16 * j + 16)
            part = slice(16 * q, 16 * q + 16)
            far = slice(TILE + 128 * q + 16 * j, TILE + 128 * q + 16 * j + 16)
            jr[rows, :] = RATE * gr_ref[j ^ my_z, part, :] + scale * (gp1_ref[rows, :] + gp2_ref[rows, :])
            jc[rows, :] = RATE * gc_ref[j ^ my_xc, part, :] + scale * (gp1_ref[far, :] + gp2_ref[far, :])
    wide_r = lax.dot_general(jr[...], inv, NT, precision=HIGHEST, preferred_element_type=F32)
    wide_ct = lax.dot_general(inv, jc[...], NT, precision=HIGHEST, preferred_element_type=F32)
    taken = jnp.dot(wide_r, wide_ct, precision=HIGHEST, preferred_element_type=F32)
    out_ref[...] = RATE * prec_ref[...] + scale * (g1_ref[...] + g2_ref[...]) - taken
    panel_mean = jnp.where(here == 1, near_ref[0, 17:18, :], far_ref[0, 17:18, :])
    mean_p = RATE * panel_mean + mean_scale * jnp.sum(fit[TILE : TILE + PB].T, axis=0, keepdims=True)
    mean_mid = RATE * mo_ref[...] + mean_scale * jnp.sum(fit[0:TILE].T, axis=0, keepdims=True)
    head = lax.dot_general(mean_p, inv, NT, precision=HIGHEST, preferred_element_type=F32)
    mean_ref[...] = mean_mid - lax.dot_general(head, wide_r, NT, precision=HIGHEST, preferred_element_type=F32)
    for h in range(2):
        span = slice(h * PB, h * PB + PB)

        @pl.when((in_col == 1) & (half == h))
        def _():
            out_ref[:, span] = wide_r

        @pl.when((in_row == 1) & (half == h))
        def _():
            out_ref[span, :] = wide_ct
            mean_ref[:, span] = head

        @pl.when((in_row == 1) & (in_col == 1) & (half == h))
        def _():
            out_ref[span, span] = low_ref[...]


def finish(idx, *args):
    vmem = pl.BlockSpec(memory_space=pltpu.VMEM)
    return pl.pallas_call(
        finish_kernel,
        in_specs=[pl.BlockSpec(memory_space=pltpu.SMEM)] + [vmem] * len(args),
        out_specs=[vmem, vmem],
        out_shape=[jax.ShapeDtypeStruct((TILE, TILE), F32), jax.ShapeDtypeStruct((1, TILE), F32)],
        scratch_shapes=[pltpu.VMEM((TILE, PB), F32), pltpu.VMEM((TILE, PB), F32)],
        compiler_params=pltpu.CompilerParams(vmem_limit_bytes=48 * 1024 * 1024),
        cost_estimate=pl.CostEstimate(flops=4_000_000_000, bytes_accessed=4_000_000, transcendentals=1000),
        name="finish",
    )(idx, *args)


def local(pool, targets, picks, inducing, inv_sq_lengths, prec_old, mean_old, panel):
    my_row = lax.axis_index(ROW)
    my_col = lax.axis_index(COL)
    my_z = lax.axis_index("z")
    my_x = lax.axis_index("x")
    my_core = lax.axis_index("core")
    my_yl = lax.axis_index("yl")
    owner = panel[0] // 2
    half = panel[0] - 2 * owner
    o_yh, o_x, o_core = owner // 8, (owner // 2) % 4, owner % 2
    o_yl, o_z = owner // 8, owner % 8
    o_xy = (o_yh * 4 + o_x) * 2 + o_yl

    def ints(*values):
        lanes = jnp.arange(len(values), dtype=jnp.int32)
        out = jnp.zeros(len(values), jnp.int32)
        for k, v in enumerate(values):
            out = jnp.where(lanes == k, v.astype(jnp.int32), out)
        return out

    z_out = pack(ints(half, my_z), picks, pool, targets, prec_old)
    z_in = lax.all_to_all(z_out, "z", 0, 0, tiled=True)
    t_rows = trace_rows(inducing, inv_sq_lengths, z_out)

    xy_out, chunk = relay(ints(o_z, half, my_z), z_in, t_rows, mean_old)
    xy_in = lax.all_to_all(xy_out, XY, 0, 0, tiled=True)
    chunk = jnp.where(my_yl == o_yl, chunk, swapped(chunk, "yl", 2, 1))
    xy_in, chunk = lax.optimization_barrier((xy_in, chunk))

    chosen = lax.dynamic_index_in_dim(xy_in, o_xy, 0, keepdims=False).astype(F32)
    trace_xy = jnp.sum(xy_in[:, 133:136].astype(F32), axis=(0, 1))
    diagonal = chosen[136] + chosen[137]
    mine = jnp.concatenate(
        [
            jnp.concatenate([chosen[160:176] + chosen[192:208], chosen[144:160] + chosen[176:192]], axis=1),
            jnp.concatenate([trace_xy, diagonal])[None, :],
            (chosen[129:131] + chosen[131:133]).reshape(1, PB),
            jnp.zeros((6, PB), F32),
        ],
        axis=0,
    )
    near = lax.all_to_all(jnp.broadcast_to(mine[None], (8, 24, PB)), "z", 0, 0, tiled=True)
    core_out = jnp.concatenate([xy_in[:, :128].reshape(HALF, 128), xy_in[:, 128]], axis=0)
    core_in = swapped(core_out, "core", 2, 1)
    crossed = lax.ppermute(chunk, ALL, [(16 * i + j, 16 * j + i) for i in range(16) for j in range(16)])
    far_r = swapped(chunk, "z", 8, 4)
    xy_in, crossed = lax.optimization_barrier((xy_in, crossed))
    two_c = jnp.stack([crossed, swapped(crossed, "core", 2, 1)])
    idx = ints(my_row, my_col, panel[0])
    part1 = gram_part(
        idx,
        inducing,
        inv_sq_lengths,
        xy_in,
        pl.BlockSpec((4, 128, 128), lambda i, idx: (i, 0, 0)),
        pl.BlockSpec((16, 16, 128), lambda i, idx: (0, 8, 0)),
    )
    part1, near, core_in, far_r, two_c, chunk = lax.optimization_barrier(
        (part1, near, core_in, far_r, two_c, chunk)
    )

    far = swapped(near, "core", 2, 1)
    two_r = jnp.stack([chunk, far_r])
    two_r = jnp.stack([two_r, swapped(two_r, "z", 8, 2)], axis=1)
    four_c = jnp.stack([two_c, swapped(two_c, "x", 4, 1)])
    part2 = gram_part(
        idx,
        inducing,
        inv_sq_lengths,
        core_in,
        pl.BlockSpec((CHUNK, 128), lambda i, idx: (i, 0)),
        pl.BlockSpec((16, 128), lambda i, idx: (HALF // 16, 0)),
    )
    part1, part2, near, far, two_r, four_c = lax.optimization_barrier((part1, part2, near, far, two_r, four_c))

    got_r = jnp.stack([two_r, swapped(two_r, "z", 8, 1)], axis=2)
    got_c = jnp.stack([four_c, swapped(four_c, "x", 4, 2)])
    here = my_core == o_core
    factor, inv_factor = factored(ints(here), near, far, part1[1], part2[1])
    updated, mean_next = finish(
        ints(my_z, 2 * my_x + my_core, half, my_row == owner, my_col == owner, here),
        near,
        far,
        mean_old.reshape(1, TILE),
        factor,
        inv_factor,
        part1[0],
        part2[0],
        part1[1],
        part2[1],
        part1[2],
        part2[2],
        got_r.reshape(8, 64, PB),
        got_c.reshape(8, 64, PB),
        prec_old,
    )
    return (updated, mean_next.reshape(TILE))


def solution(mesh):
    split = Mesh(mesh.devices.reshape(2, 4, 2, 2, 8), ALL)
    return jax.shard_map(
        local,
        mesh=split,
        in_specs=(P(ALL, None), P(ALL), P(ALL), P(), P(), P(ROW, COL), P(ROW), P()),
        out_specs=(P(ROW, COL), P(ROW)),
        check_vma=False,
    )
```

```python
import functools
import math

import jax
import jax.numpy as jnp
from jax import lax
from jax.experimental import pallas as pl
from jax.experimental.pallas import tpu as pltpu
from jax.sharding import Mesh
from jax.sharding import PartitionSpec as P

M = 8192
F = 128
PB = 256
TILE = 512
B_TOTAL = 4096
HALF = 2048
CHUNK = 512
ROW = ("yh", "x", "core")
COL = ("yl", "z")
XY = ("yh", "x", "yl")
ALL = ROW + COL
RATE = 0.5
EPSILON = 1e-05
LOG2E = math.log2(math.e)
F32 = jnp.float32
BF16 = jnp.bfloat16
NT = (((1,), (1,)), ((), ()))
HIGHEST = lax.Precision.HIGHEST


def swapped(value, axis, size, bit):
    return lax.ppermute(value, axis, [(i, i ^ bit) for i in range(size)])


def split2(value):
    high = lax.reduce_precision(value, 8, 7)
    return high.astype(BF16), (value - high).astype(BF16)


def split3(value):
    high = lax.reduce_precision(value, 8, 7)
    rest = value - high
    mid = lax.reduce_precision(rest, 8, 7)
    return high.astype(BF16), mid.astype(BF16), (rest - mid).astype(BF16)


def pieces(value):
    high = value.astype(BF16)
    rest = value - high.astype(F32)
    mid = rest.astype(BF16)
    return high, mid, (rest - mid.astype(F32)).astype(BF16)


def scaled_points(pts, w):
    scaled = pts * w * LOG2E
    high = scaled.astype(BF16)
    low = (scaled - high.astype(F32)).astype(BF16)
    return high, low, jnp.sum(pts * pts * w, axis=1, keepdims=True) * (-0.5 * LOG2E)


def sample_terms(x, w):
    xf = x.astype(F32)
    return jnp.sum((xf * xf * w).T, axis=0, keepdims=True) * (-0.5 * LOG2E)


def split_rows(out, at, n, value):
    high = value.astype(BF16)
    low = (value - high.astype(F32)).astype(BF16)
    for k, part in enumerate((high[:, :128], high[:, 128:], low[:, :128], low[:, 128:])):
        out[at + k * n : at + (k + 1) * n, :] = part


def pack_kernel(idx_ref, picks_ref, pool_ref, targets_ref, prec_ref, out_ref):
    sub = lax.broadcasted_iota(jnp.int32, (16, 128), 0)
    lane = lax.broadcasted_iota(jnp.int32, (16, 128), 1)
    at = jnp.zeros((16, 128), jnp.int32)
    for n in range(16):
        at = jnp.where(sub == n, picks_ref[n], at)
    hot = jnp.where(at == lane, 1.0, 0.0)
    samples = jnp.dot(hot.astype(BF16), pool_ref[...], preferred_element_type=F32).astype(BF16)
    y = jnp.sum(hot * targets_ref[...].astype(F32), axis=1, keepdims=True)
    y_row = jnp.sum(jnp.where(lane == 16 * idx_ref[1] + sub, y, 0.0), axis=0, keepdims=True)
    y_rows = jnp.where(sub == 0, y_row, 0.0).astype(BF16)
    for j in range(8):
        chunk = jnp.concatenate([prec_ref[128 * q + 16 * j : 128 * q + 16 * j + 16, :] for q in range(4)], axis=0)
        split_rows(out_ref.at[j], 0, 64, chunk)
        out_ref[j, 256:272, :] = samples
        out_ref[j, 272:288, :] = y_rows


def pack(idx, picks, pool, targets, prec_old):
    return pl.pallas_call(
        pack_kernel,
        grid_spec=pltpu.PrefetchScalarGridSpec(
            num_scalar_prefetch=2,
            grid=(1,),
            in_specs=[
                pl.BlockSpec((128, 128), lambda i, idx, picks: (0, 0)),
                pl.BlockSpec((1, 128), lambda i, idx, picks: (0, 0)),
                pl.BlockSpec((TILE, PB), lambda i, idx, picks: (0, idx[0])),
            ],
            out_specs=pl.BlockSpec((8, 288, 128), lambda i, idx, picks: (0, 0, 0)),
        ),
        out_shape=jax.ShapeDtypeStruct((8, 288, 128), BF16),
        compiler_params=pltpu.CompilerParams(vmem_limit_bytes=12 * 1024 * 1024),
        name="pack",
    )(idx, picks, pool, targets[None, :], prec_old)


def trace_kernel(ind_ref, w_ref, x_ref, out_ref, paug, xaug, total):
    step = pl.program_id(0)
    w = w_ref[...]
    x = x_ref[0]

    @pl.when(step == 0)
    def _():
        total[...] = jnp.zeros_like(total)
        xaug[:, 0:128] = x
        xaug[:, 128:256] = x

    high, low, own = scaled_points(ind_ref[...], w)
    paug[:, 0:128] = high
    paug[:, 128:256] = low
    e = lax.dot_general(paug[...], xaug[...], NT, preferred_element_type=F32)
    f = jnp.exp2(e + own + sample_terms(x, w)).astype(BF16).astype(F32)
    total[:, 0:16] += jnp.sum((f * f).reshape(128, 8, 16), axis=0)

    @pl.when(step == pl.num_programs(0) - 1)
    def _():
        sub = lax.broadcasted_iota(jnp.int32, (16, 128), 0)
        h, m, l = (p.astype(F32) for p in pieces(jnp.sum(total[...], axis=0, keepdims=True)))
        out_ref[...] = jnp.where(sub == 0, h, jnp.where(sub == 1, m, jnp.where(sub == 2, l, 0.0))).astype(BF16)


def trace_rows(inducing, weights, packed):
    return pl.pallas_call(
        trace_kernel,
        grid=(M // 1024,),
        in_specs=[
            pl.BlockSpec((1024, F), lambda i: (i, 0)),
            pl.BlockSpec((1, F), lambda i: (0, 0)),
            pl.BlockSpec((1, 16, F), lambda i: (0, 16, 0)),
        ],
        out_specs=pl.BlockSpec((16, 128), lambda i: (0, 0)),
        out_shape=jax.ShapeDtypeStruct((16, 128), BF16),
        scratch_shapes=[pltpu.VMEM((1024, 256), BF16), pltpu.VMEM((16, 256), BF16), pltpu.VMEM((8, 128), F32)],
        cost_estimate=pl.CostEstimate(flops=4_000_000_000, bytes_accessed=4_000_000, transcendentals=1_000_000),
        compiler_params=pltpu.CompilerParams(vmem_limit_bytes=16 * 1024 * 1024),
        name="trace_rows",
    )(inducing, weights[None, :], packed)


def relay_kernel(idx_ref, z_ref, t_ref, mean_ref, out_ref, chunk_ref):
    src, half, my_z = idx_ref[0], idx_ref[1], idx_ref[2]
    sub = lax.broadcasted_iota(jnp.int32, (16, 128), 0)
    lane = lax.broadcasted_iota(jnp.int32, (16, 128), 1)
    values = z_ref[src, 0:256, :].astype(F32)
    chunk_ref[:, 0:128] = values[0:64] + values[128:192]
    chunk_ref[:, 128:256] = values[64:128] + values[192:256]
    parts, diagonals = [], []
    for k in range(2):
        left, right = values[128 * k : 128 * k + 64], values[128 * k + 64 : 128 * k + 128]
        top = jnp.where(half == 0, left[0:16], left[32:48])
        low_left = jnp.where(half == 0, left[16:32], left[48:64])
        low_right = jnp.where(half == 0, right[16:32], right[48:64])
        own = 16 * my_z + sub
        parts += [low_left, jnp.where(lane <= own, top, low_right)]
        diagonals.append(jnp.sum(jnp.where(lane == own, low_right, 0.0), axis=0, keepdims=True))
    y = jnp.sum(z_ref[:, 272:288, :].astype(F32), axis=0)
    means = mean_ref[pl.ds(2 * half, 2), :]
    m_high = means.astype(BF16).astype(F32)
    m_low = means - m_high
    t = t_ref[...].astype(F32)
    aux = jnp.where(sub == 0, y, 0.0)
    rows = (m_high[0:1], m_high[1:2], m_low[0:1], m_low[1:2], t[0:1], t[1:2], t[2:3], *diagonals)
    for k, row in enumerate(rows):
        aux = jnp.where(sub == k + 1, row, aux)
    whole = jnp.concatenate([p.astype(BF16) for p in (aux, *parts)], axis=0)
    samples = z_ref[:, 256:272, :].reshape(128, 128)
    for k in range(16):
        out_ref[k, 0:128, :] = samples
        out_ref[k, 128:208, :] = whole


def relay(idx, z_in, t_rows, mean_old):
    vmem = pl.BlockSpec(memory_space=pltpu.VMEM)
    return pl.pallas_call(
        relay_kernel,
        in_specs=[pl.BlockSpec(memory_space=pltpu.SMEM), vmem, vmem, vmem],
        out_specs=[vmem, vmem],
        out_shape=[jax.ShapeDtypeStruct((16, 208, 128), BF16), jax.ShapeDtypeStruct((64, PB), F32)],
        compiler_params=pltpu.CompilerParams(vmem_limit_bytes=12 * 1024 * 1024),
        name="relay",
    )(idx, z_in, t_rows, mean_old.reshape(4, 128))


def gram_kernel(idx_ref, pr_ref, pc_ref, pp_ref, w_ref, x_ref, y_ref, grc_ref, gp_ref, gpp_ref, fit_ref, paug, own, xaug, ys):
    step = pl.program_id(0)

    @pl.when(step == 0)
    def _():
        at = 0
        for ref in (pr_ref, pc_ref, pp_ref):
            n = ref.shape[0]
            high, low, term = scaled_points(ref[...], w_ref[...])
            paug[at : at + n, 0:128] = high
            paug[at : at + n, 128:256] = low
            own[at : at + n, :] = jnp.broadcast_to(term, (n, 128))
            at += n
        y_all = (y_ref[:, 0, :] if len(y_ref.shape) == 3 else y_ref[...]).astype(F32)
        for k in range(4):
            ys[k, 0:4, :] = y_all[4 * k : 4 * k + 4]
        grc_ref[...] = jnp.zeros_like(grc_ref)
        gp_ref[...] = jnp.zeros_like(gp_ref)
        gpp_ref[...] = jnp.zeros_like(gpp_ref)
        fit_ref[...] = jnp.zeros_like(fit_ref)
        fit_ref[TILE + PB : TILE + PB + 1, :] = jnp.sum(y_all * y_all, axis=0, keepdims=True)

    x = x_ref[...].reshape(CHUNK, F)
    xaug[:, 0:128] = x
    xaug[:, 128:256] = x
    xa = xaug[...]
    sample_term = sample_terms(x, w_ref[...])

    def feats(at, n):
        e = lax.dot_general(paug[at : at + n, :], xa, NT, preferred_element_type=F32)
        term = own[at : at + n, :]
        e = e + jnp.concatenate([term] * (CHUNK // 128), axis=1) + sample_term
        return jnp.exp2(e).astype(BF16)

    f_r = feats(0, TILE)
    f_c = feats(TILE, TILE)
    f_p = feats(2 * TILE, PB)
    grc_ref[...] += lax.dot_general(f_r, f_c, NT, preferred_element_type=F32)
    gp_ref[0:TILE, :] += lax.dot_general(f_r, f_p, NT, preferred_element_type=F32)
    gp_ref[TILE : 2 * TILE, :] += lax.dot_general(f_c, f_p, NT, preferred_element_type=F32)
    gpp_ref[...] += lax.dot_general(f_p, f_p, NT, preferred_element_type=F32)
    y = ys[step]
    for at, f in ((0, f_r), (TILE, f_p)):
        acc = fit_ref[at : at + f.shape[0], :]
        for k in range(CHUNK // 128):
            acc = acc + f[:, 128 * k : 128 * (k + 1)].astype(F32) * y[k : k + 1, :]
        fit_ref[at : at + f.shape[0], :] = acc


def gram_part(idx, inducing, weights, source, x_spec, y_spec):
    shapes = ((TILE, TILE), (2 * TILE, PB), (PB, PB), (TILE + PB + 8, 128))
    return pl.pallas_call(
        gram_kernel,
        grid_spec=pltpu.PrefetchScalarGridSpec(
            num_scalar_prefetch=1,
            grid=(HALF // CHUNK,),
            in_specs=[
                pl.BlockSpec((TILE, F), lambda i, idx: (idx[0], 0)),
                pl.BlockSpec((TILE, F), lambda i, idx: (idx[1], 0)),
                pl.BlockSpec((PB, F), lambda i, idx: (idx[2], 0)),
                pl.BlockSpec((1, F), lambda i, idx: (0, 0)),
                x_spec,
                y_spec,
            ],
            out_specs=[pl.BlockSpec(s, lambda i, idx: (0, 0)) for s in shapes],
            scratch_shapes=[
                pltpu.VMEM((2 * TILE + PB, 256), BF16),
                pltpu.VMEM((2 * TILE + PB, 128), F32),
                pltpu.VMEM((CHUNK, 256), BF16),
                pltpu.VMEM((4, 8, 128), F32),
            ],
        ),
        out_shape=[jax.ShapeDtypeStruct(s, F32) for s in shapes],
        compiler_params=pltpu.CompilerParams(vmem_limit_bytes=28 * 1024 * 1024),
        cost_estimate=pl.CostEstimate(flops=12_000_000_000, bytes_accessed=8_000_000, transcendentals=2_600_000),
        name="gram_part",
    )(idx, inducing, inducing, inducing, weights[None, :], source, source)


def trace_scale_of(near_ref, far_ref):
    traces = jnp.zeros((1, 128), F32)
    for j in range(8):
        traces = traces + (near_ref[j, 16:17, 0:128] + far_ref[j, 16:17, 0:128])
    return jnp.sum(traces, axis=1, keepdims=True) * (1.0 / M)


def factor_kernel(idx_ref, near_ref, far_ref, gp1_ref, gp2_ref, low_ref, inv_ref, work, cols, dinv, mrow):
    here = idx_ref[0] == 1
    row_id = lax.broadcasted_iota(jnp.int32, (PB, PB), 0)
    col_id = lax.broadcasted_iota(jnp.int32, (PB, PB), 1)
    low = lax.broadcasted_iota(jnp.int32, (128, 128), 0)
    lane = lax.broadcasted_iota(jnp.int32, (128, 128), 1)
    scale = RATE / trace_scale_of(near_ref, far_ref)
    blocks = [jnp.where(here, near_ref[j], far_ref[j]) for j in range(8)]
    both = jnp.concatenate([b[0:16, 0:128] for b in blocks], axis=0)
    low_left = jnp.concatenate([b[0:16, 128:256] for b in blocks], axis=0)
    diagonal = jnp.concatenate([jnp.broadcast_to(b[16:17, 128:256], (16, 128)) for b in blocks], axis=0)
    on = low == lane
    under = jnp.where(low > lane, both, 0.0)
    over = jnp.where(low < lane, both, 0.0)
    gram = scale * (gp1_ref[...] + gp2_ref[...])
    work[0:128, 0:128] = RATE * (under + under.T + jnp.where(on, both, 0.0)) + gram[0:128, 0:128]
    work[0:128, 128:256] = RATE * low_left.T + gram[0:128, 128:256]
    work[128:256, 0:128] = RATE * low_left + gram[128:256, 0:128]
    work[128:256, 128:256] = RATE * (over + over.T + jnp.where(on, diagonal, 0.0)) + gram[128:256, 128:256]
    work[:, PB:] = jnp.where(row_id == col_id, 1.0, 0.0)
    for b in range(PB // 8):
        base = 8 * b
        tile = base // 128 * 128
        spans = [t for t in range(0, 2 * PB, 128) if (tile <= t < PB) or PB <= t <= PB + base]
        d8 = work[base : base + 8, tile : tile + 128]
        for k in range(8):
            cols[8 * k : 8 * k + 8, :] = jnp.broadcast_to(d8[:, base - tile + k : base - tile + k + 1], (8, 128))
        d = {(i, k): cols[8 * k + i : 8 * k + i + 1, :] for k in range(8) for i in range(k, 8)}
        lo = {}
        rs = {}
        m = {}
        for k in range(8):
            rs[k] = lax.rsqrt(d[k, k])
            for i in range(k + 1, 8):
                lo[i, k] = d[i, k] * rs[k]
            for i in range(k + 1, 8):
                for j in range(k + 1, i + 1):
                    d[i, j] = d[i, j] - lo[i, k] * lo[j, k]
            m[k, k] = rs[k]
            for j in range(k):
                acc = lo[k, j] * m[j, j]
                for t in range(j + 1, k):
                    acc = acc + lo[k, t] * m[t, j]
                m[k, j] = -acc * rs[k]
        zero = jnp.zeros((1, 128), F32)
        for j in range(8):
            for i in range(8):
                mrow[8 * j + i : 8 * j + i + 1, :] = m[i, j] if i >= j else zero
        for i in range(8):
            for j in range(i, 8):
                acc = m[j, i] * m[j, j]
                for t in range(j + 1, 8):
                    acc = acc + m[t, i] * m[t, j]
                dinv[8 * j + i : 8 * j + i + 1, :] = acc
                if i != j:
                    dinv[8 * i + j : 8 * i + j + 1, :] = acc
        t_rows = {}
        for s in spans:
            u = None
            tt = None
            for j in range(8):
                r = work[base + j : base + j + 1, s : s + 128]
                if b + 1 < PB // 8:
                    q = dinv[8 * j : 8 * j + 8, :] * r
                    tt = q if tt is None else tt + q
                q = mrow[8 * j : 8 * j + 8, :] * r
                u = q if u is None else u + q
            t_rows[s] = tt
            work[base : base + 8, s : s + 128] = u
        for s in spans:
            if t_rows[s] is not None:
                cols[64 + 8 * (s // 128) : 72 + 8 * (s // 128), :] = t_rows[s]
        for g in range(b + 1, PB // 8):
            rows = slice(8 * g, 8 * g + 8)
            a = work[rows, tile : tile + 128]
            coef = [jnp.broadcast_to(a[:, base - tile + k : base - tile + k + 1], (8, 128)) for k in range(8)]
            for s in spans:
                v = work[rows, s : s + 128]
                for k in range(8):
                    v = v - coef[k] * cols[64 + 8 * (s // 128) + k : 65 + 8 * (s // 128) + k, :]
                work[rows, s : s + 128] = v
    low_ref[...] = jnp.where(row_id >= col_id, work[:, 0:PB].T, 0.0)
    inv_ref[...] = jnp.where(row_id >= col_id, work[:, PB:], 0.0)


def factored(idx, near, far, gp1, gp2):
    vmem = pl.BlockSpec(memory_space=pltpu.VMEM)
    shape = jax.ShapeDtypeStruct((PB, PB), F32)
    return pl.pallas_call(
        factor_kernel,
        in_specs=[pl.BlockSpec(memory_space=pltpu.SMEM), vmem, vmem, vmem, vmem],
        out_specs=[vmem, vmem],
        out_shape=[shape, shape],
        scratch_shapes=[
            pltpu.VMEM((PB, 2 * PB), F32),
            pltpu.VMEM((96, 128), F32),
            pltpu.VMEM((64, 128), F32),
            pltpu.VMEM((64, 128), F32),
        ],
        cost_estimate=pl.CostEstimate(flops=16_000_000_000, bytes_accessed=1_000_000, transcendentals=1000),
        compiler_params=pltpu.CompilerParams(vmem_limit_bytes=12 * 1024 * 1024),
        name="factored",
    )(idx, near, far, gp1, gp2)


def finish_kernel(
    idx_ref, near_ref, far_ref, mo_ref, low_ref, inv_ref, g1_ref, g2_ref, gp1_ref, gp2_ref, fit1_ref, fit2_ref,
    gr_ref, hr_ref, gc_ref, hc_ref, prec_ref, out_ref, mean_ref, jr, jc,
):
    my_z, my_xc, half, in_row, in_col, here = (idx_ref[k] for k in range(6))
    trace_scale = trace_scale_of(near_ref, far_ref)
    scale = RATE / trace_scale
    fit = fit1_ref[...] + fit2_ref[...]
    power = jnp.sum(fit[TILE + PB : TILE + PB + 1, :], axis=1, keepdims=True)
    mean_scale = RATE / jnp.sqrt(trace_scale * (power * (1.0 / B_TOTAL) + EPSILON))
    inv = inv_ref[...]
    for j in range(8):
        at_r, at_c = j ^ my_z, j ^ my_xc
        from_r = jnp.where(at_r % 2 == 0, gr_ref[at_r // 2], hr_ref[at_r // 2])
        from_c = jnp.where(at_c < 4, gc_ref[at_c % 4], hc_ref[at_c % 4])
        for q in range(4):
            rows = slice(128 * q + 16 * j, 128 * q + 16 * j + 16)
            part = slice(16 * q, 16 * q + 16)
            far = slice(TILE + 128 * q + 16 * j, TILE + 128 * q + 16 * j + 16)
            jr[rows, :] = RATE * from_r[part] + scale * (gp1_ref[rows, :] + gp2_ref[rows, :])
            jc[rows, :] = RATE * from_c[part] + scale * (gp1_ref[far, :] + gp2_ref[far, :])
    wide_r = lax.dot_general(jr[...], inv, NT, precision=HIGHEST, preferred_element_type=F32)
    wide_ct = lax.dot_general(inv, jc[...], NT, precision=HIGHEST, preferred_element_type=F32)
    taken = jnp.dot(wide_r, wide_ct, precision=HIGHEST, preferred_element_type=F32)
    out_ref[...] = RATE * prec_ref[...] + scale * (g1_ref[...] + g2_ref[...]) - taken
    panel_mean = jnp.where(here == 1, near_ref[0, 17:18, :], far_ref[0, 17:18, :])
    mean_p = RATE * panel_mean + mean_scale * jnp.sum(fit[TILE : TILE + PB].T, axis=0, keepdims=True)
    mean_mid = RATE * mo_ref[...] + mean_scale * jnp.sum(fit[0:TILE].T, axis=0, keepdims=True)
    head = lax.dot_general(mean_p, inv, NT, precision=HIGHEST, preferred_element_type=F32)
    mean_ref[...] = mean_mid - lax.dot_general(head, wide_r, NT, precision=HIGHEST, preferred_element_type=F32)
    for h in range(2):
        span = slice(h * PB, h * PB + PB)

        @pl.when((in_col == 1) & (half == h))
        def _():
            out_ref[:, span] = wide_r

        @pl.when((in_row == 1) & (half == h))
        def _():
            out_ref[span, :] = wide_ct
            mean_ref[:, span] = head

        @pl.when((in_row == 1) & (in_col == 1) & (half == h))
        def _():
            out_ref[span, span] = low_ref[...]


def finish(idx, *args):
    vmem = pl.BlockSpec(memory_space=pltpu.VMEM)
    return pl.pallas_call(
        finish_kernel,
        in_specs=[pl.BlockSpec(memory_space=pltpu.SMEM)] + [vmem] * len(args),
        out_specs=[vmem, vmem],
        out_shape=[jax.ShapeDtypeStruct((TILE, TILE), F32), jax.ShapeDtypeStruct((1, TILE), F32)],
        scratch_shapes=[pltpu.VMEM((TILE, PB), F32), pltpu.VMEM((TILE, PB), F32)],
        compiler_params=pltpu.CompilerParams(vmem_limit_bytes=28 * 1024 * 1024),
        cost_estimate=pl.CostEstimate(flops=4_000_000_000, bytes_accessed=4_000_000, transcendentals=1000),
        name="finish",
    )(idx, *args)


def local(pool, targets, picks, inducing, inv_sq_lengths, prec_old, mean_old, panel):
    my_row = lax.axis_index(ROW)
    my_col = lax.axis_index(COL)
    my_z = lax.axis_index("z")
    my_x = lax.axis_index("x")
    my_core = lax.axis_index("core")
    my_yl = lax.axis_index("yl")
    owner = panel[0] // 2
    half = panel[0] - 2 * owner
    o_yh, o_x, o_core = owner // 8, (owner // 2) % 4, owner % 2
    o_yl, o_z = owner // 8, owner % 8
    o_xy = (o_yh * 4 + o_x) * 2 + o_yl

    def ints(*values):
        lanes = jnp.arange(len(values), dtype=jnp.int32)
        out = jnp.zeros(len(values), jnp.int32)
        for k, v in enumerate(values):
            out = jnp.where(lanes == k, v.astype(jnp.int32), out)
        return out

    z_out = pack(ints(half, my_z), picks, pool, targets, prec_old)
    z_in = lax.all_to_all(z_out, "z", 0, 0, tiled=True)
    t_rows = trace_rows(inducing, inv_sq_lengths, z_out)

    xy_out, chunk = relay(ints(o_z, half, my_z), z_in, t_rows, mean_old)
    xy_in = lax.all_to_all(xy_out, XY, 0, 0, tiled=True)
    chunk = jnp.where(my_yl == o_yl, chunk, swapped(chunk, "yl", 2, 1))
    crossed = lax.ppermute(chunk, ALL, [(16 * i + j, 16 * j + i) for i in range(16) for j in range(16)])
    far_r = swapped(chunk, "z", 8, 4)

    chosen = lax.dynamic_index_in_dim(xy_in, o_xy, 0, keepdims=False).astype(F32)
    trace_xy = jnp.sum(xy_in[:, 133:136].astype(F32), axis=(0, 1))
    diagonal = chosen[136] + chosen[137]
    mine = jnp.concatenate(
        [
            jnp.concatenate([chosen[160:176] + chosen[192:208], chosen[144:160] + chosen[176:192]], axis=1),
            jnp.concatenate([trace_xy, diagonal])[None, :],
            (chosen[129:131] + chosen[131:133]).reshape(1, PB),
            jnp.zeros((6, PB), F32),
        ],
        axis=0,
    )
    near = lax.all_to_all(jnp.broadcast_to(mine[None], (8, 24, PB)), "z", 0, 0, tiled=True)
    core_out = jnp.concatenate([xy_in[:, :128].reshape(HALF, 128), xy_in[:, 128]], axis=0)
    core_in = swapped(core_out, "core", 2, 1)
    xy_in, crossed = lax.optimization_barrier((xy_in, crossed))
    two_c = jnp.stack([crossed, swapped(crossed, "core", 2, 1)])
    idx = ints(my_row, my_col, panel[0])
    part1 = gram_part(
        idx,
        inducing,
        inv_sq_lengths,
        xy_in,
        pl.BlockSpec((4, 128, 128), lambda i, idx: (i, 0, 0)),
        pl.BlockSpec((16, 16, 128), lambda i, idx: (0, 8, 0)),
    )
    part1, near, core_in, far_r, two_c, chunk = lax.optimization_barrier(
        (part1, near, core_in, far_r, two_c, chunk)
    )

    far = swapped(near, "core", 2, 1)
    two_r = jnp.stack([chunk, far_r])
    two_r = jnp.stack([two_r, swapped(two_r, "z", 8, 2)], axis=1).reshape(4, 64, PB)
    four_c = jnp.stack([two_c, swapped(two_c, "x", 4, 1)])
    part2 = gram_part(
        idx,
        inducing,
        inv_sq_lengths,
        core_in,
        pl.BlockSpec((CHUNK, 128), lambda i, idx: (i, 0)),
        pl.BlockSpec((16, 128), lambda i, idx: (HALF // 16, 0)),
    )
    four_c = four_c.reshape(4, 64, PB)
    part1, part2, near, far, two_r, four_c = lax.optimization_barrier((part1, part2, near, far, two_r, four_c))

    more_r = swapped(two_r, "z", 8, 1)
    more_c = swapped(four_c, "x", 4, 2)
    here = my_core == o_core
    factor, inv_factor = factored(ints(here), near, far, part1[2], part2[2])
    updated, mean_next = finish(
        ints(my_z, 2 * my_x + my_core, half, my_row == owner, my_col == owner, here),
        near,
        far,
        mean_old.reshape(1, TILE),
        factor,
        inv_factor,
        part1[0],
        part2[0],
        part1[1],
        part2[1],
        part1[3],
        part2[3],
        two_r,
        more_r,
        four_c,
        more_c,
        prec_old,
    )
    return (updated, mean_next.reshape(TILE))


def solution(mesh):
    split = Mesh(mesh.devices.reshape(2, 4, 2, 2, 8), ALL)
    return jax.shard_map(
        local,
        mesh=split,
        in_specs=(P(ALL, None), P(ALL), P(ALL), P(), P(), P(ROW, COL), P(ROW), P()),
        out_specs=(P(ROW, COL), P(ROW)),
        check_vma=False,
    )
```
